128 devices in a mesh: dp: 8 (over x, y_hi), shard: 16 (over y_lo, z, core).
Axes of the slice: x: 4, y: 4 (y_hi: 2, y_lo: 2; y = y_hi * 2 + y_lo), z: 4, core: 2. Of those that a mesh axis runs over, the one named last changes fastest.
Arguments:
- frames: bfloat16 [1024, 64, 1536], P(('dp', 'shard')), may hold values from -24 to 24
- cotangent: bfloat16 [1024, 64, 1536], P(('dp', 'shard')), may hold values from -24 to 24
- lengths: int32 [1024], P(('dp', 'shard')), may hold values from 1 to 64, 49152 in all
- send_order: int32 [1024], P(('dp', 'shard')), may hold values from 0 to 7, as said below
- norm_gain: bfloat16 [1536], P('shard'), may hold values from 0.099609375 to 1.8984375
- conv_bias: bfloat16 [1536], P('shard'), may hold values from -3 to 3
- kernel: bfloat16 [1536, 31], P('shard'), may hold values from -1 to 1
- expand_weight: bfloat16 [1536, 3072], P('shard'), may hold values from -0.15625 to 0.15625
- project_weight: bfloat16 [1536, 1536], P('shard'), may hold values from -0.15625 to 0.15625
Outputs:
- encoded: bfloat16 [1024, 64, 1536], P(('dp', 'shard'))
- frame_grad: bfloat16 [1024, 64, 1536], P(('dp', 'shard'))
- gain_grad: float32 [1536], P('shard')
- bias_grad: float32 [1536], P('shard')
- kernel_grad: float32 [1536, 31], P('shard')
- expand_grad: float32 [1536, 3072], P('shard')
- project_grad: float32 [1536, 1536], P('shard')
The draws below stay inside these ranges and needn't reach their ends.
Inputs may be any that keep to these rules, and one draw needn't show every extreme that they name: `send_order`: each aligned block of 8 entries, the utterances of one device, is a permutation of 0 to 7. `lengths`: at least one utterance has exactly 64 live frames.
All inputs are finite; a program needn't handle non-finite values. No bound on the sum of `lengths` on one device may be relied on, other than what follows from the above.
Results may differ from the reference program's by a relative error of at most 0.03.
Values may be sent and summed in bfloat16 or wider, within the bound.
A program may use at most 128 MiB of HBM per device.

```python
import math
import jax
import jax.numpy as jnp
import numpy as np
from jax import lax

D = 1536
KW = 31
L = 64
UPEER = 1
U_DEV = 8
UTT = 1024
N_DP = 8
N_SHARD = 16


def draw_send_order(key, part):
    split_keys = jax.random.split(key, UTT // U_DEV)
    blocks = jax.vmap(lambda single: jax.random.permutation(single, U_DEV))(split_keys)
    return blocks.reshape(UTT).astype(jnp.int32)


def raised(entries, rng, source, target, blocks, factor):
    def block_of(axis_at):
        return (jnp.arange(entries.shape[axis_at]) // (entries.shape[axis_at] // blocks)).reshape((-1,) + (1,) * (entries.ndim - 1 - axis_at))

    first = jax.random.permutation(rng, blocks)[block_of(target)]
    other_side = (block_of(target) + blocks // 2) % blocks
    return jnp.where((block_of(source) == first) | (block_of(source) == other_side), factor * entries, entries)


def level_of(key, shape, cuts, smallest, top_value):
    factor_of, own = 1.0, jax.random.fold_in(key, 6)
    for axis_at, blocks in cuts:
        heights = jnp.exp(jax.random.uniform(jax.random.fold_in(own, axis_at), (blocks,), jnp.float32, smallest / len(cuts), top_value / len(cuts)))
        factor_of = factor_of * jnp.repeat(heights, shape[axis_at] // blocks).reshape([-1 if axis == axis_at else 1 for axis in range(len(shape))])
    return factor_of


def split_up(amount, total, limit, lean):
    weights = [(1 << 20) // math.isqrt(rank ** lean) + 1 for rank in range(2, amount + 1)]
    rest, counts = total - limit - (amount - 1), [1] * (amount - 1)
    while rest > 0:
        free = [i for i in range(amount - 1) if counts[i] < limit]
        pool, budget = sum([weights[i] for i in free]), rest
        for i in free:
            more = min(limit - counts[i], max(1, budget * weights[i] // pool), rest)
            counts[i] = counts[i] + more
            rest = rest - more
    return np.array([limit] + counts)


def ragged_sizes(key, number_of, total, limit, lean):
    if number_of == 2:
        one = jax.random.randint(key, (), max(1, total - limit), min(limit, total - 1) + 1)
        return jnp.stack([one, total - one])
    tallies = jnp.asarray(split_up(number_of, total, limit, lean), jnp.int32)
    pairs = (number_of - 1) // 2
    donor, receiver = tallies[1:1 + 2 * pairs:2], tallies[2:2 + 2 * pairs:2]
    margin = jnp.minimum(donor - 1, limit - receiver)
    moved = jax.random.randint(jax.random.fold_in(key, 1), (pairs,), 0, 1 << 20) % (margin + 1)
    tallies = tallies.at[1:1 + 2 * pairs:2].set(donor - moved).at[2:2 + 2 * pairs:2].set(receiver + moved)
    return tallies[jax.random.permutation(jax.random.fold_in(key, 2), number_of)]


def bell_draw(stream_key, dims, spread, bound, cuts=(), kind=jnp.bfloat16):
    level = level_of(stream_key, dims, cuts, -0.22, 0.18) if cuts else 1.0
    drawn = jax.random.normal(stream_key, dims, jnp.float32) * spread * level
    return jnp.minimum(jnp.maximum(drawn, -bound), bound).astype(kind)


def noise_with(stream_key, extent, scale, limit, cuts, heavy, kind=jnp.bfloat16):
    entries = scale * jax.random.normal(stream_key, extent, jnp.float32)
    if cuts:
        entries = entries * level_of(stream_key, extent, cuts, -0.22, 0.18)
    return jnp.clip(raised(entries, jax.random.fold_in(stream_key, 3), *heavy), -limit, limit).astype(kind)


def setup_inputs(seed: int = 0) -> dict:
    streams_of = jax.random.split(jax.random.key(seed), 10)
    frames = noise_with(streams_of[0], (UTT, L, D), 1.0, 24.0, ((0, 128),), (0, 2, 128, 5.5))
    cotangent = noise_with(streams_of[1], (UTT, L, D), 1.0, 24.0, ((0, 128),), (0, 2, 128, 5.5))
    lengths = ragged_sizes(streams_of[2], UTT, UTT * L * 3 // 4, L, 1).astype(jnp.int32)
    send_order = draw_send_order(jax.random.fold_in(streams_of[9], 71), 0)
    norm_gain = jnp.clip(1.0 + 0.18 * jax.random.normal(streams_of[4], (D,), jnp.float32), 0.099609375, 1.8984375).astype(jnp.bfloat16)
    conv_bias = bell_draw(streams_of[5], (D,), 0.5, 3.0, ((0, 16),))
    kernel = bell_draw(streams_of[6], (D, KW), KW ** -0.5, 1.0, ((0, 16),))
    expand_weight = bell_draw(streams_of[7], (D, 2 * D), D ** -0.5, 0.15625, ((0, 16),))
    project_weight = bell_draw(streams_of[8], (D, D), D ** -0.5, 0.15625, ((0, 16),))
    return {"frames": frames, "cotangent": cotangent, "lengths": lengths, "send_order": send_order, "norm_gain": norm_gain, "conv_bias": conv_bias, "kernel": kernel, "expand_weight": expand_weight, "project_weight": project_weight}


EPS = 1e-05

def depthwise(signal, taps_table):
    taps = taps_table.shape[1]
    half = (taps - 1) // 2
    length = signal.shape[1]
    padded = jnp.pad(signal, ((0, 0), (half, half), (0, 0)))
    result = jnp.zeros_like(signal)
    for offset in range(taps):
        result = result + padded[:, offset:offset + length, :] * taps_table[:, offset]
    return result

def kernel_terms(signal, upstream, taps):
    half = (taps - 1) // 2
    length = signal.shape[1]
    padded = jnp.pad(signal, ((0, 0), (half, half), (0, 0)))
    columns = []
    for offset in range(taps):
        columns.append(lax.optimization_barrier(jnp.sum(padded[:, offset:offset + length, :] * upstream, axis=(0, 1))))
    return jnp.stack(columns, axis=1)

def block_local(frames, cotangent, live, norm_gain, conv_bias, kernel, expand_weight, project_weight):
    count, length, width = frames.shape
    total_rows = count * length
    inputs = frames.reshape(total_rows, width).astype(jnp.float32)
    live_rows = live.reshape(total_rows, 1)
    centre = lax.optimization_barrier(jnp.mean(inputs, axis=1, keepdims=True))
    centred = inputs - centre
    variance = lax.optimization_barrier(jnp.mean(centred * centred, axis=1, keepdims=True))
    inverse = lax.rsqrt(variance + EPS)
    standard = centred * inverse
    complete_gain = norm_gain.astype(jnp.float32)
    normed = (standard * complete_gain).astype(jnp.bfloat16)
    expanded = jnp.dot(normed, expand_weight, preferred_element_type=jnp.float32)
    value_portion = expanded[:, :width]
    gate_sig = jax.nn.sigmoid(expanded[:, width:])
    glu_out = (value_portion * gate_sig * live_rows).astype(jnp.bfloat16)
    taps_full = kernel.astype(jnp.float32)
    glu_cube = glu_out.astype(jnp.float32).reshape(count, length, width)
    conv_out = depthwise(glu_cube, taps_full).reshape(total_rows, width) + conv_bias.astype(jnp.float32)
    conv_sig = jax.nn.sigmoid(conv_out)
    swished = (conv_out * conv_sig).astype(jnp.bfloat16)
    projected = jnp.dot(swished, project_weight, preferred_element_type=jnp.float32)
    encoded = (inputs + projected * live_rows).astype(jnp.bfloat16)
    upstream = cotangent.reshape(total_rows, width).astype(jnp.float32)
    masked = (upstream * live_rows).astype(jnp.bfloat16)
    project_part = jnp.dot(swished.T, masked, preferred_element_type=jnp.float32)
    grad_swish = jnp.dot(masked, project_weight.T, preferred_element_type=jnp.float32)
    grad_conv = grad_swish * conv_sig * (1.0 + conv_out * (1.0 - conv_sig))
    bias_portion = lax.optimization_barrier(jnp.sum(grad_conv, axis=0))
    gradient_volume = grad_conv.reshape(count, length, width)
    kernel_part = kernel_terms(glu_cube, gradient_volume, kernel.shape[1])
    grad_glu = depthwise(gradient_volume, taps_full[:, ::-1]).reshape(total_rows, width) * live_rows
    grad_expanded = jnp.concatenate([grad_glu * gate_sig, grad_glu * value_portion * gate_sig * (1.0 - gate_sig)], axis=1).astype(jnp.bfloat16)
    expand_part = jnp.dot(normed.T, grad_expanded, preferred_element_type=jnp.float32)
    grad_normed = jnp.dot(grad_expanded, expand_weight.T, preferred_element_type=jnp.float32)
    gain_part = lax.optimization_barrier(jnp.sum(grad_normed * standard, axis=0))
    grad_standard = grad_normed * complete_gain
    grad_inputs = inverse * (grad_standard - lax.optimization_barrier(jnp.mean(grad_standard, axis=1, keepdims=True)) - standard * lax.optimization_barrier(jnp.mean(grad_standard * standard, axis=1, keepdims=True)))
    frame_grad = (upstream + grad_inputs).astype(jnp.bfloat16)
    return (encoded.reshape(count, length, width), frame_grad.reshape(count, length, width), (gain_part, bias_portion, kernel_part, expand_part, project_part))

def reference(frames, cotangent, lengths, send_order, norm_gain, conv_bias, kernel, expand_weight, project_weight):
    balanced = jnp.arange(UTT, dtype=jnp.int32)
    device = balanced // U_DEV
    within = balanced % U_DEV
    target_dp = device // N_SHARD
    shard_pos = device % N_SHARD
    source_dp = within // UPEER
    slot_pos = within % UPEER
    source_device = source_dp * N_SHARD + shard_pos
    source = source_device * U_DEV + jnp.take(send_order, source_device * U_DEV + target_dp * UPEER + slot_pos)
    frames_bal = jnp.take(frames, source, axis=0)
    cot_bal = jnp.take(cotangent, source, axis=0)
    length_bal = jnp.take(lengths, source)
    positions = lax.broadcasted_iota(jnp.int32, (UTT, L), 1)
    live = (positions < length_bal[:, None]).astype(jnp.float32)
    devices_all = N_DP * N_SHARD
    zeros_init = (jnp.zeros((D,), jnp.float32), jnp.zeros((D,), jnp.float32), jnp.zeros((D, KW), jnp.float32), jnp.zeros((D, 2 * D), jnp.float32), jnp.zeros((D, D), jnp.float32))

    def device_step(running, pieces):
        enc_part, gradient_portion, parts = block_local(pieces[0], pieces[1], pieces[2], norm_gain, conv_bias, kernel, expand_weight, project_weight)
        rounded = lax.optimization_barrier(tuple((part.astype(jnp.bfloat16) for part in parts)))
        updated_params = tuple((total + piece.astype(jnp.float32) for total, piece in zip(running, rounded)))
        return (updated_params, (enc_part, gradient_portion))
    totals, outputs = lax.scan(device_step, zeros_init, (frames_bal.reshape(devices_all, U_DEV, L, D), cot_bal.reshape(devices_all, U_DEV, L, D), live.reshape(devices_all, U_DEV, L)))
    encoded = outputs[0].reshape(UTT, L, D)
    frame_grad = jnp.zeros((UTT, L, D), jnp.bfloat16).at[source].set(outputs[1].reshape(UTT, L, D))
    return (encoded, frame_grad, totals[0], totals[1], totals[2], totals[3], totals[4])
```

```python
import jax
import jax.numpy as jnp
from jax import lax
from jax.experimental import pallas as pl
from jax.experimental.pallas import tpu as pltpu
from jax.sharding import PartitionSpec as P

EPS = 1e-05
MESH = pl.DeviceIdType.MESH
D, L, U, ROWS = 1536, 64, 8, 96
JOBW, JOBS = 768, 6
f32, bf16 = jnp.float32, jnp.bfloat16


class Place:
    def __init__(self):
        self.dp, self.sh = lax.axis_index("dp"), lax.axis_index("shard")
        self.x, self.yh = self.dp // 2, lax.rem(self.dp, 2)
        self.yl = self.sh // 8
        self.z = lax.rem(self.sh, 8) // 2
        self.c = lax.rem(self.sh, 2)
        self.zp, self.zm, self.z2 = (lax.rem(self.z + k, 4) for k in (1, 3, 2))
        y = self.yh * 2 + self.yl
        other = 1 - self.yl

        def at_y(step):
            return (self.x * 2 + lax.rem(y + step, 4) // 2, other * 8 + self.z * 2 + self.c)

        self.up, self.down = at_y(1), at_y(3)
        self.fore = (self.dp, self.yl * 8 + self.zp * 2 + self.c)
        self.back = (self.dp, self.yl * 8 + self.zm * 2 + self.c)
        self.sib = (self.dp, self.yl * 8 + self.z * 2 + 1 - self.c)
        self.pair = (self.x * 2 + 1 - self.yh, self.sh)

    def dp_peer(self, step):
        return (lax.rem(self.dp + step, 8), self.sh)

    def x_peer(self, step):
        return (lax.rem(self.x + step, 4) * 2 + self.yh, self.sh)

    def shard_of(self, yl, z, c):
        return yl * 8 + z * 2 + c

    def greet(self):
        barrier = pltpu.get_barrier_semaphore()
        peers = [self.up, self.down, self.fore, self.back, self.sib] + [self.dp_peer(k) for k in range(1, 8)]
        for peer in peers:
            pl.semaphore_signal(barrier, inc=1, device_id=peer, device_id_type=MESH)
        pl.semaphore_wait(barrier, len(peers))


def remote(src, dst, send, recv, peer):
    return pltpu.make_async_remote_copy(
        src_ref=src, dst_ref=dst, send_sem=send, recv_sem=recv, device_id=peer, device_id_type=MESH
    )


class Gather:
    def __init__(self, at, block, rows, send, recv, job):
        self.p, self.block, self.rows = at, block, rows
        self.s, self.r = (lambda k: send.at[job, k]), (lambda k: recv.at[job, k])
        self.a, self.b, self.full = (0, rows // 2), (rows // 2, rows // 2), (0, rows)
        self.sent = []

    def push(self, shard, part, sem, peer):
        ref = self.block(shard, *part)
        copy = remote(ref, ref, self.s(sem), self.r(sem), peer)
        copy.start()
        self.sent.append(copy)

    def arrive(self, shard, part, sem):
        ref = self.block(shard, *part)
        remote(ref, ref, self.s(sem), self.r(sem), self.p.sib).wait_recv()

    def step(self, n):
        p = self.p
        own, opp = p.yl, 1 - p.yl
        if n == 0:
            mine = p.sh
            self.push(mine, self.a, 0, p.up)
            self.push(mine, self.b, 1, p.down)
            self.push(mine, self.full, 2, p.fore)
            self.push(mine, self.full, 3, p.back)
            self.push(mine, self.full, 10, p.sib)
        elif n == 1:
            j = p.shard_of(opp, p.z, p.c)
            self.arrive(j, self.a, 0)
            self.arrive(j, self.b, 1)
            self.push(j, self.full, 4, p.fore)
            self.push(j, self.full, 5, p.back)
            self.push(j, self.full, 11, p.sib)
        elif n in (2, 3):
            yl, k, f, s = (own, 2, 6, 12) if n == 2 else (opp, 4, 8, 14)
            m, q = p.shard_of(yl, p.zm, p.c), p.shard_of(yl, p.zp, p.c)
            self.arrive(m, self.full, k)
            self.push(m, self.a, f, p.fore)
            self.push(m, self.full, s, p.sib)
            self.arrive(q, self.full, k + 1)
            self.push(q, self.b, f + 1, p.back)
            self.push(q, self.full, s + 1, p.sib)
        elif n == 4:
            for yl, k, s in ((own, 6, 16), (opp, 8, 17)):
                j = p.shard_of(yl, p.z2, p.c)
                self.arrive(j, self.a, k)
                self.arrive(j, self.b, k + 1)
                self.push(j, self.full, s, p.sib)
        else:
            d = 1 - p.c
            order = ((own, p.z), (opp, p.z), (own, p.zm), (own, p.zp), (opp, p.zm), (opp, p.zp), (own, p.z2), (opp, p.z2))
            for k, (yl, z) in enumerate(order):
                self.arrive(p.shard_of(yl, z, d), self.full, 10 + k)

    def drain(self):
        for copy in self.sent:
            copy.wait_send()


def exchange(at, src, dst, send, recv):
    copies = []
    for k in range(1, 8):
        peer = at.dp_peer(k)
        copy = remote(src.at[peer[0]], dst.at[at.dp], send.at[k], recv.at[k], peer)
        copy.start()
        copies.append(copy)
    own = pltpu.make_async_copy(src.at[at.dp], dst.at[at.dp], send.at[0])
    own.start()
    return copies, own


def exchange_wait(at, src, dst, send, recv, started):
    copies, own = started
    own.wait()
    for k in range(1, 8):
        remote(src.at[at.dp], dst.at[lax.rem(at.dp + 8 - k, 8)], send.at[k], recv.at[k], at.sib).wait_recv()


def entry_kernel(
    frames, cot, lens, small, expand, project,
    o_frames, o_cot, o_lens, o_small, o_expand, o_project,
    xs, xr, gs, gr, local,
):
    at = Place()
    places = [
        (small, o_small.at[at.sh]),
        (expand, o_expand.at[at.sh]),
        (project, o_project.at[at.sh]),
    ]
    fills = [pltpu.make_async_copy(s, d, local.at[k]) for k, (s, d) in enumerate(places)]
    for fill in fills:
        fill.start()
    at.greet()
    arrays = ((lens, o_lens), (frames, o_frames), (cot, o_cot))
    started = [exchange(at, s, d, xs.at[k], xr.at[k]) for k, (s, d) in enumerate(arrays[:2])]
    for fill in fills:
        fill.wait()

    def block_small(j, start, size):
        return o_small.at[j, pl.ds(start, size), :]

    def block_of(out, col):
        return lambda j, start, size: out.at[j, pl.ds(start, size), pl.ds(col, JOBW)]

    jobs = [Gather(at, block_small, 48, gs, gr, 0)]
    for k in range(4):
        jobs.append(Gather(at, block_of(o_expand, k * JOBW), ROWS, gs, gr, 1 + k))
    for k in range(2):
        jobs.append(Gather(at, block_of(o_project, k * JOBW), ROWS, gs, gr, 5 + k))
    for job in jobs:
        job.step(0)
    started.append(exchange(at, cot, o_cot, xs.at[2], xr.at[2]))
    for n in range(1, 6):
        for job in jobs:
            job.step(n)
    for k, (s, d) in enumerate(arrays):
        exchange_wait(at, s, d, xs.at[k], xr.at[k], started[k])
    for copies, _ in started:
        for copy in copies:
            copy.wait_send()
    for job in jobs:
        job.drain()


def entry(frames, cot, lens, small, expand, project):
    any_spec = pl.BlockSpec(memory_space=pl.ANY)
    dma = pltpu.SemaphoreType.DMA
    shapes = [
        jax.ShapeDtypeStruct((U, L, D), bf16),
        jax.ShapeDtypeStruct((U, L, D), bf16),
        jax.ShapeDtypeStruct((U, 8, 128), jnp.int32),
        jax.ShapeDtypeStruct((16, 48, 128), f32),
        jax.ShapeDtypeStruct((16, ROWS, 2 * D), bf16),
        jax.ShapeDtypeStruct((16, ROWS, D), bf16),
    ]
    return pl.pallas_call(
        entry_kernel,
        out_shape=shapes,
        in_specs=[any_spec] * 6,
        out_specs=[any_spec] * 6,
        scratch_shapes=[dma((3, 8)), dma((3, 8)), dma((7, 18)), dma((7, 18)), dma((3,))],
        compiler_params=pltpu.CompilerParams(collective_id=0, has_side_effects=True),
    )(frames, cot, lens, small, expand, project)


def blocks_add(rows, pieces, out):
    step = 16

    @pl.loop(0, rows // step)
    def _(k):
        span = pl.ds(pl.multiple_of(k * step, step), step)
        total = pieces[0][span, :].astype(f32)
        for piece in pieces[1:]:
            total = total + piece[span, :].astype(f32)
        out[span, :] = total.astype(out.dtype)


class Reduce:
    def __init__(self, at, job, part, b, sems):
        self.p, self.job, self.part, self.b = at, job, part, b
        self.send, self.recv = sems
        self.sent = []

    def push(self, src, dst, sem, peer):
        copy = remote(src, dst, self.send.at[self.job, sem], self.recv.at[self.job, sem], peer)
        copy.start()
        self.sent.append(copy)

    def arrive(self, ref, sem):
        remote(ref, ref, self.send.at[self.job, sem], self.recv.at[self.job, sem], self.p.sib).wait_recv()

    def piece(self, ref, q):
        return ref.at[pl.ds((q // 2) * 48, 48), pl.ds(pl.multiple_of(lax.rem(q, 2) * 384, 128), 384)]

    def step(self, n):
        p, k = self.p, self.job
        own, sibr, za, zb, yr, xr, xs, hr, fin, out, local = (
            self.b[name] for name in ("own", "sib", "za", "zb", "yr", "xr", "xs", "hr", "fin", "out", "local")
        )
        own, sibr, za, zb, yr, xr, xs, hr, fin = (r.at[k] for r in (own, sibr, za, zb, yr, xr, xs, hr, fin))
        if n == 0:
            self.push(self.part(1 - p.c), sibr, 0, p.sib)
            pltpu.make_async_copy(self.part(p.c), own, local.at[k]).start()
        elif n == 1:
            pltpu.make_async_copy(self.part(p.c), own, local.at[k]).wait()
            self.arrive(sibr, 0)
            for yl in range(2):
                for z in range(4):
                    blocks_add(ROWS, [own.at[yl, z], sibr.at[yl, z]], own.at[yl, z])
            self.push(own.at[:, p.z2, 0:48], za.at[0], 1, p.fore)
            self.push(own.at[:, p.z2, 48:96], za.at[1], 2, p.back)
        elif n == 2:
            self.arrive(za.at[0], 1)
            for yl in range(2):
                half = own.at[yl, p.zp, 0:48]
                blocks_add(48, [half, za.at[0, yl]], half)
            self.push(own.at[:, p.zp], zb.at[0], 3, p.fore)
            self.arrive(za.at[1], 2)
            for yl in range(2):
                half = own.at[yl, p.zm, 48:96]
                blocks_add(48, [half, za.at[1, yl]], half)
            self.push(own.at[:, p.zm], zb.at[1], 4, p.back)
        elif n == 3:
            self.arrive(zb.at[0], 3)
            self.arrive(zb.at[1], 4)
            for yl in range(2):
                mine = own.at[yl, p.z]
                blocks_add(ROWS, [mine, zb.at[0, yl], zb.at[1, yl]], mine)
            theirs = own.at[1 - p.yl, p.z]
            self.push(theirs.at[0:48], yr.at[0:48], 5, p.up)
            self.push(theirs.at[48:96], yr.at[48:96], 6, p.down)
        elif n == 4:
            self.arrive(yr.at[0:48], 5)
            self.arrive(yr.at[48:96], 6)
            mine = own.at[p.yl, p.z]
            blocks_add(ROWS, [mine, yr], mine)
            for s in range(1, 4):
                self.push(self.piece(mine, lax.rem(p.x + s, 4)), xr.at[s - 1], 6 + s, p.x_peer(s))
        elif n == 5:
            for s in range(1, 4):
                self.arrive(xr.at[s - 1], 6 + s)
            blocks_add(48, [self.piece(own.at[p.yl, p.z], p.x), xr.at[0], xr.at[1], xr.at[2]], xs)
            self.push(xs, hr, 10, p.pair)
        elif n == 6:
            self.arrive(hr, 10)
            mine = self.piece(fin, p.x)
            blocks_add(48, [xs, hr], mine)
            for s in range(1, 4):
                self.push(mine, mine, 10 + s, p.x_peer(s))
        else:
            for s in range(1, 4):
                self.arrive(self.piece(fin, lax.rem(p.x + 4 - s, 4)), 10 + s)
            blocks_add(ROWS, [fin], out(k))

    def drain(self):
        for copy in self.sent:
            copy.wait_send()


class ReduceSmall:
    def __init__(self, at, part, b, send, recv):
        self.p, self.part, self.b, self.send, self.recv = at, part, b, send, recv
        self.sent = []

    def push(self, src, dst, sem, peer):
        copy = remote(src, dst, self.send.at[sem], self.recv.at[sem], peer)
        copy.start()
        self.sent.append(copy)

    def arrive(self, ref, sem):
        remote(ref, ref, self.send.at[sem], self.recv.at[sem], self.p.sib).wait_recv()

    def step(self, n):
        p, b = self.p, self.b
        own, sibr, za, zb, yr, dr, out = (b[name] for name in ("own", "sib", "za", "zb", "yr", "dr", "out"))
        if n == 0:
            self.push(self.part.at[:, :, 1 - p.c], sibr, 0, p.sib)
        elif n == 1:
            self.arrive(sibr, 0)
            for yl in range(2):
                for z in range(4):
                    own[yl, z] = self.part[yl, z, p.c] + sibr[yl, z]
            self.push(own.at[:, p.z2, 0:24], za.at[0], 1, p.fore)
            self.push(own.at[:, p.z2, 24:48], za.at[1], 2, p.back)
        elif n == 2:
            self.arrive(za.at[0], 1)
            self.arrive(za.at[1], 2)
            for yl in range(2):
                own[yl, p.zp, 0:24] = own[yl, p.zp, 0:24] + za[0, yl]
                own[yl, p.zm, 24:48] = own[yl, p.zm, 24:48] + za[1, yl]
            self.push(own.at[:, p.zp], zb.at[0], 3, p.fore)
            self.push(own.at[:, p.zm], zb.at[1], 4, p.back)
        elif n == 3:
            self.arrive(zb.at[0], 3)
            self.arrive(zb.at[1], 4)
            for yl in range(2):
                own[yl, p.z] = own[yl, p.z] + zb[0, yl] + zb[1, yl]
            theirs = own.at[1 - p.yl, p.z]
            self.push(theirs.at[0:24], yr.at[0:24], 5, p.up)
            self.push(theirs.at[24:48], yr.at[24:48], 6, p.down)
        elif n == 4:
            self.arrive(yr.at[0:24], 5)
            self.arrive(yr.at[24:48], 6)
            dr[p.dp] = own[p.yl, p.z] + yr[...]
            for s in range(1, 8):
                self.push(dr.at[p.dp], dr.at[p.dp], 6 + s, p.dp_peer(s))
        elif n == 5:
            for s in range(1, 8):
                self.arrive(dr.at[lax.rem(p.dp + 8 - s, 8)], 6 + s)
            total = dr[0]
            for s in range(1, 8):
                total = total + dr[s]
            out[...] = total

    def drain(self):
        for copy in self.sent:
            copy.wait_send()


def exit_kernel(
    grad, small, expand, project,
    o_grad, o_small, o_expand, o_project,
    own, sibr, za, zb, yr, xr, xsum, hr, fin,
    sown, ssib, sza, szb, syr, sdr,
    xs, xrv, rs, rr, ss, sr, local,
):
    at = Place()
    at.greet()
    started = exchange(at, grad, o_grad, xs, xrv)

    def part_of(ref, col):
        return lambda c: ref.at[:, :, c, :, pl.ds(col, JOBW)]

    def out(k):
        return o_project.at[:, k * JOBW : (k + 1) * JOBW] if k < 2 else o_expand.at[:, (k - 2) * JOBW : (k - 1) * JOBW]

    bufs = {
        "own": own, "sib": sibr, "za": za, "zb": zb, "yr": yr, "xr": xr, "xs": xsum, "hr": hr,
        "fin": fin, "out": out, "local": local,
    }
    parts = [part_of(project, k * JOBW) for k in range(2)] + [part_of(expand, k * JOBW) for k in range(4)]
    jobs = [Reduce(at, k, parts[k], bufs, (rs, rr)) for k in range(JOBS)]
    tiny = ReduceSmall(
        at, small, {"own": sown, "sib": ssib, "za": sza, "zb": szb, "yr": syr, "dr": sdr, "out": o_small}, ss, sr
    )
    for job in jobs:
        job.step(0)
    tiny.step(0)
    for n in range(1, JOBS + 7):
        for k in range(JOBS):
            stage = n - k
            if 1 <= stage <= 7:
                jobs[k].step(stage)
        if n <= 5:
            tiny.step(n)
    exchange_wait(at, grad, o_grad, xs, xrv, started)
    for copy in started[0]:
        copy.wait_send()
    for job in jobs:
        job.drain()
    tiny.drain()


def leave(grad, small, expand, project):
    any_spec = pl.BlockSpec(memory_space=pl.ANY)
    vmem = pl.BlockSpec(memory_space=pltpu.VMEM)
    dma = pltpu.SemaphoreType.DMA
    shapes = [
        jax.ShapeDtypeStruct((U, L, D), bf16),
        jax.ShapeDtypeStruct((48, 128), f32),
        jax.ShapeDtypeStruct((ROWS, 2 * D), f32),
        jax.ShapeDtypeStruct((ROWS, D), f32),
    ]
    V = pltpu.VMEM
    return pl.pallas_call(
        exit_kernel,
        out_shape=shapes,
        in_specs=[any_spec, vmem, any_spec, any_spec],
        out_specs=[any_spec, vmem, vmem, vmem],
        scratch_shapes=[
            V((JOBS, 2, 4, ROWS, JOBW), bf16),
            V((JOBS, 2, 4, ROWS, JOBW), bf16),
            V((JOBS, 2, 2, 48, JOBW), bf16),
            V((JOBS, 2, 2, ROWS, JOBW), bf16),
            V((JOBS, ROWS, JOBW), bf16),
            V((JOBS, 3, 48, 384), bf16),
            V((JOBS, 48, 384), bf16),
            V((JOBS, 48, 384), bf16),
            V((JOBS, ROWS, JOBW), bf16),
            V((2, 4, 48, 128), f32),
            V((2, 4, 48, 128), f32),
            V((2, 2, 24, 128), f32),
            V((2, 2, 48, 128), f32),
            V((48, 128), f32),
            V((8, 48, 128), f32),
            dma((8,)), dma((8,)), dma((JOBS, 14)), dma((JOBS, 14)), dma((14,)), dma((14,)), dma((JOBS,)),
        ],
        compiler_params=pltpu.CompilerParams(
            collective_id=1, has_side_effects=True, vmem_limit_bytes=60 * 1024 * 1024
        ),
    )(grad, small.reshape(2, 4, 2, 48, 128), expand.reshape(2, 4, 2, ROWS, 2 * D), project.reshape(2, 4, 2, ROWS, D))


def depthwise(signal, taps_table):
    taps = taps_table.shape[1]
    half = (taps - 1) // 2
    length = signal.shape[1]
    padded = jnp.pad(signal, ((0, 0), (half, half), (0, 0)))
    result = jnp.zeros_like(signal)
    for offset in range(taps):
        result = result + padded[:, offset : offset + length, :] * taps_table[:, offset]
    return result


def kernel_terms(signal, upstream, taps):
    half = (taps - 1) // 2
    length = signal.shape[1]
    padded = jnp.pad(signal, ((0, 0), (half, half), (0, 0)))
    columns = []
    for offset in range(taps):
        columns.append(jnp.sum(padded[:, offset : offset + length, :] * upstream, axis=(0, 1)))
    return jnp.stack(columns, axis=1)


def block_local(frames, cotangent, live, norm_gain, conv_bias, kernel, expand_weight, project_weight):
    count, length, width = frames.shape
    total_rows = count * length
    inputs = frames.reshape(total_rows, width).astype(f32)
    live_rows = live.reshape(total_rows, 1)
    centre = jnp.mean(inputs, axis=1, keepdims=True)
    centred = inputs - centre
    variance = jnp.mean(centred * centred, axis=1, keepdims=True)
    inverse = lax.rsqrt(variance + EPS)
    standard = centred * inverse
    complete_gain = norm_gain.astype(f32)
    normed = (standard * complete_gain).astype(bf16)
    expanded = jnp.dot(normed, expand_weight, preferred_element_type=f32)
    value_portion = expanded[:, :width]
    gate_sig = jax.nn.sigmoid(expanded[:, width:])
    glu_out = (value_portion * gate_sig * live_rows).astype(bf16)
    taps_full = kernel.astype(f32)
    glu_cube = glu_out.astype(f32).reshape(count, length, width)
    conv_out = depthwise(glu_cube, taps_full).reshape(total_rows, width) + conv_bias.astype(f32)
    conv_sig = jax.nn.sigmoid(conv_out)
    swished = (conv_out * conv_sig).astype(bf16)
    projected = jnp.dot(swished, project_weight, preferred_element_type=f32)
    encoded = (inputs + projected * live_rows).astype(bf16)
    upstream = cotangent.reshape(total_rows, width).astype(f32)
    masked = (upstream * live_rows).astype(bf16)
    project_part = jnp.dot(swished.T, masked, preferred_element_type=f32)
    grad_swish = jnp.dot(masked, project_weight.T, preferred_element_type=f32)
    grad_conv = grad_swish * conv_sig * (1.0 + conv_out * (1.0 - conv_sig))
    bias_portion = jnp.sum(grad_conv, axis=0)
    gradient_volume = grad_conv.reshape(count, length, width)
    kernel_part = kernel_terms(glu_cube, gradient_volume, kernel.shape[1])
    grad_glu = depthwise(gradient_volume, taps_full[:, ::-1]).reshape(total_rows, width) * live_rows
    grad_expanded = jnp.concatenate(
        [grad_glu * gate_sig, grad_glu * value_portion * gate_sig * (1.0 - gate_sig)], axis=1
    ).astype(bf16)
    expand_part = jnp.dot(normed.T, grad_expanded, preferred_element_type=f32)
    grad_normed = jnp.dot(grad_expanded, expand_weight.T, preferred_element_type=f32)
    gain_part = jnp.sum(grad_normed * standard, axis=0)
    grad_standard = grad_normed * complete_gain
    grad_inputs = inverse * (
        grad_standard
        - jnp.mean(grad_standard, axis=1, keepdims=True)
        - standard * jnp.mean(grad_standard * standard, axis=1, keepdims=True)
    )
    frame_grad = (upstream + grad_inputs).astype(bf16)
    return (
        encoded.reshape(count, length, width),
        frame_grad.reshape(count, length, width),
        (gain_part, bias_portion, kernel_part, expand_part, project_part),
    )


def body(frames, cotangent, lengths, send_order, norm_gain, conv_bias, kernel, expand_weight, project_weight):
    count, length, width = frames.shape
    staged_frames = frames.at[send_order].get(mode="promise_in_bounds")
    staged_cot = cotangent.at[send_order].get(mode="promise_in_bounds")
    staged_len = jnp.broadcast_to(lengths.at[send_order].get(mode="promise_in_bounds")[:, None, None], (U, 8, 128))
    small = jnp.concatenate([kernel.T, norm_gain[None], conv_bias[None]], axis=0).astype(f32)
    small = jnp.pad(small, ((0, 48 - 33), (0, 128 - ROWS)))
    r_frames, r_cot, r_len, r_small, r_expand, r_project = entry(
        staged_frames, staged_cot, staged_len, small, expand_weight, project_weight
    )
    positions = lax.broadcasted_iota(jnp.int32, (count, length), 1)
    live = (positions < r_len[:, 0, :1]).astype(f32)
    table = r_small[:, :33, :ROWS].transpose(0, 2, 1).reshape(D, 33)
    encoded, balanced_grad, parts = block_local(
        r_frames, r_cot, live, table[:, 31], table[:, 32], table[:, :31],
        r_expand.reshape(D, 2 * D), r_project.reshape(D, D),
    )
    rows = jnp.concatenate([parts[2].T, parts[0][None], parts[1][None]], axis=0)
    rows = rows.astype(bf16).astype(f32)
    small_part = jnp.pad(rows.reshape(33, 16, ROWS).transpose(1, 0, 2), ((0, 0), (0, 15), (0, 128 - ROWS)))
    returned, g_small, g_expand, g_project = leave(
        balanced_grad, small_part, parts[3].astype(bf16), parts[4].astype(bf16)
    )
    plan = (send_order[None, :] == lax.broadcasted_iota(jnp.int32, (count, count), 0)).astype(bf16)
    frame_grad = jnp.einsum("kp,pfh->kfh", plan, returned, preferred_element_type=f32).astype(bf16)
    return (
        encoded, frame_grad, g_small[31, :ROWS], g_small[32, :ROWS], g_small[:31, :ROWS].T, g_expand, g_project,
    )


def solution(mesh):
    both, shard = P(("dp", "shard"), None, None), P("shard", None)
    return jax.shard_map(
        body,
        mesh=mesh,
        in_specs=(both, both, P(("dp", "shard")), P(("dp", "shard")), P("shard"), P("shard"), shard, shard, shard),
        out_specs=(both, both, P("shard"), P("shard"), shard, shard, shard),
        check_vma=False,
    )
```

```python
import jax
import jax.numpy as jnp
from jax import lax
from jax.experimental import pallas as pl
from jax.experimental.pallas import tpu as pltpu
from jax.sharding import PartitionSpec as P

EPS = 1e-05
MESH = pl.DeviceIdType.MESH
D, L, U, ROWS = 1536, 64, 8, 96
JOBW, JOBS, TILE, TILES, TAPS, HALF = 768, 6, 384, 4, 31, 15
N = U * L
f32, bf16 = jnp.float32, jnp.bfloat16


class Place:
    def __init__(self):
        self.dp, self.sh = lax.axis_index("dp"), lax.axis_index("shard")
        self.x, self.yh = self.dp // 2, lax.rem(self.dp, 2)
        self.yl = self.sh // 8
        self.z = lax.rem(self.sh, 8) // 2
        self.c = lax.rem(self.sh, 2)
        self.zp, self.zm, self.z2 = (lax.rem(self.z + k, 4) for k in (1, 3, 2))
        y = self.yh * 2 + self.yl
        other = 1 - self.yl

        def at_y(step):
            return (self.x * 2 + lax.rem(y + step, 4) // 2, other * 8 + self.z * 2 + self.c)

        self.up, self.down = at_y(1), at_y(3)
        self.fore = (self.dp, self.yl * 8 + self.zp * 2 + self.c)
        self.back = (self.dp, self.yl * 8 + self.zm * 2 + self.c)
        self.sib = (self.dp, self.yl * 8 + self.z * 2 + 1 - self.c)
        self.pair = (self.x * 2 + 1 - self.yh, self.sh)

    def dp_peer(self, step):
        return (lax.rem(self.dp + step, 8), self.sh)

    def x_peer(self, step):
        return (lax.rem(self.x + step, 4) * 2 + self.yh, self.sh)

    def shard_of(self, yl, z, c):
        return yl * 8 + z * 2 + c

    def greet(self):
        barrier = pltpu.get_barrier_semaphore()
        peers = [self.up, self.down, self.fore, self.back, self.sib] + [self.dp_peer(k) for k in range(1, 8)]
        for peer in peers:
            pl.semaphore_signal(barrier, inc=1, device_id=peer, device_id_type=MESH)
        pl.semaphore_wait(barrier, len(peers))


def remote(src, dst, send, recv, peer):
    return pltpu.make_async_remote_copy(
        src_ref=src, dst_ref=dst, send_sem=send, recv_sem=recv, device_id=peer, device_id_type=MESH
    )


class Gather:
    def __init__(self, at, block, rows, send, recv, job):
        self.p, self.block, self.rows = at, block, rows
        self.s, self.r = (lambda k: send.at[job, k]), (lambda k: recv.at[job, k])
        self.a, self.b, self.full = (0, rows // 2), (rows // 2, rows // 2), (0, rows)
        self.sent, self.done = [], 0

    def push(self, shard, part, sem, peer):
        ref = self.block(shard, *part)
        copy = remote(ref, ref, self.s(sem), self.r(sem), peer)
        copy.start()
        self.sent.append(copy)

    def arrive(self, shard, part, sem):
        ref = self.block(shard, *part)
        remote(ref, ref, self.s(sem), self.r(sem), self.p.sib).wait_recv()

    def first(self):
        self.push(self.p.sh, self.a, 0, self.p.up)
        self.push(self.p.sh, self.b, 1, self.p.down)

    def advance(self):
        if self.done < 6:
            self.step(self.done)
            self.done += 1

    def step(self, n):
        p = self.p
        own, opp = p.yl, 1 - p.yl
        if n == 0:
            self.push(p.sh, self.full, 2, p.fore)
            self.push(p.sh, self.full, 3, p.back)
            self.push(p.sh, self.full, 10, p.sib)
        elif n == 1:
            j = p.shard_of(opp, p.z, p.c)
            self.arrive(j, self.a, 0)
            self.arrive(j, self.b, 1)
            self.push(j, self.full, 4, p.fore)
            self.push(j, self.full, 5, p.back)
            self.push(j, self.full, 11, p.sib)
        elif n in (2, 3):
            yl, k, f, s = (own, 2, 6, 12) if n == 2 else (opp, 4, 8, 14)
            m, q = p.shard_of(yl, p.zm, p.c), p.shard_of(yl, p.zp, p.c)
            self.arrive(m, self.full, k)
            self.push(m, self.a, f, p.fore)
            self.push(m, self.full, s, p.sib)
            self.arrive(q, self.full, k + 1)
            self.push(q, self.b, f + 1, p.back)
            self.push(q, self.full, s + 1, p.sib)
        elif n == 4:
            for yl, k, s in ((own, 6, 16), (opp, 8, 17)):
                j = p.shard_of(yl, p.z2, p.c)
                self.arrive(j, self.a, k)
                self.arrive(j, self.b, k + 1)
                self.push(j, self.full, s, p.sib)
        else:
            d = 1 - p.c
            order = (
                (own, p.z), (opp, p.z), (own, p.zm), (own, p.zp), (opp, p.zm), (opp, p.zp), (own, p.z2), (opp, p.z2),
            )
            for k, (yl, z) in enumerate(order):
                self.arrive(p.shard_of(yl, z, d), self.full, 10 + k)

    def drain(self):
        for copy in self.sent:
            copy.wait_send()


class Exchange:
    def __init__(self, at, src, dst, send, recv):
        self.p, self.src, self.dst, self.s, self.r, self.sent = at, src, dst, send, recv, []
        for k in range(1, 8):
            peer = at.dp_peer(k)
            copy = remote(src(peer[0]), dst(at.dp), send.at[k], recv.at[k], peer)
            copy.start()
            self.sent.append(copy)
        self.own = pltpu.make_async_copy(src(at.dp), dst(at.dp), send.at[0])
        self.own.start()

    def wait(self):
        self.own.wait()
        for k in range(1, 8):
            slot = lax.rem(self.p.dp + 8 - k, 8)
            remote(self.src(slot), self.dst(slot), self.s.at[k], self.r.at[k], self.p.sib).wait_recv()

    def drain(self):
        for copy in self.sent:
            copy.wait_send()


def blocks_add(rows, pieces, out):
    step = 16

    @pl.loop(0, rows // step)
    def _(k):
        span = pl.ds(pl.multiple_of(k * step, step), step)
        total = pieces[0][span, :].astype(f32)
        for piece in pieces[1:]:
            total = total + piece[span, :].astype(f32)
        out[span, :] = total.astype(out.dtype)


OWN_RING, SEND_RING = 4, 2


class Reduce:
    def __init__(self, at, job, b, sems):
        self.p, self.job, self.b = at, job, b
        self.send, self.recv = sems
        self.sent, self.sib_sent, self.done = [], None, 0
        self.own_at, self.send_at = job % OWN_RING, OWN_RING + job % SEND_RING

    def slot(self, core):
        return self.own_at + lax.rem(core + self.p.c, 2) * (self.send_at - self.own_at)

    def push(self, src, dst, sem, peer):
        copy = remote(src, dst, self.send.at[self.job, sem], self.recv.at[self.job, sem], peer)
        copy.start()
        self.sent.append(copy)

    def arrive(self, ref, sem):
        remote(ref, ref, self.send.at[self.job, sem], self.recv.at[self.job, sem], self.p.sib).wait_recv()

    def piece(self, ref, q):
        return ref.at[pl.ds((q // 2) * 48, 48), pl.ds(pl.multiple_of(lax.rem(q, 2) * 384, 128), 384)]

    def advance(self):
        if self.done < 8:
            self.step(self.done)
            self.done += 1

    def step(self, n):
        p, k = self.p, self.job
        sibr, za, zb, yr, xr, xs, hr, fin = (self.b[m].at[k] for m in ("sib", "za", "zb", "yr", "xr", "xs", "hr", "fin"))
        own = self.b["mix"].at[self.own_at]
        if n == 0:
            self.push(self.b["mix"].at[self.send_at], sibr, 0, p.sib)
            self.sib_sent = self.sent.pop()
        elif n == 1:
            self.arrive(sibr, 0)
            for yl in range(2):
                for z in range(4):
                    blocks_add(ROWS, [own.at[yl, z], sibr.at[yl, z]], own.at[yl, z])
            self.push(own.at[:, p.z2, 0:48], za.at[0], 1, p.fore)
            self.push(own.at[:, p.z2, 48:96], za.at[1], 2, p.back)
        elif n == 2:
            self.arrive(za.at[0], 1)
            for yl in range(2):
                half = own.at[yl, p.zp, 0:48]
                blocks_add(48, [half, za.at[0, yl]], half)
            self.push(own.at[:, p.zp], zb.at[0], 3, p.fore)
            self.arrive(za.at[1], 2)
            for yl in range(2):
                half = own.at[yl, p.zm, 48:96]
                blocks_add(48, [half, za.at[1, yl]], half)
            self.push(own.at[:, p.zm], zb.at[1], 4, p.back)
        elif n == 3:
            self.arrive(zb.at[0], 3)
            self.arrive(zb.at[1], 4)
            for yl in range(2):
                mine = own.at[yl, p.z]
                blocks_add(ROWS, [mine, zb.at[0, yl], zb.at[1, yl]], mine)
            theirs = own.at[1 - p.yl, p.z]
            self.push(theirs.at[0:48], yr.at[0:48], 5, p.up)
            self.push(theirs.at[48:96], yr.at[48:96], 6, p.down)
        elif n == 4:
            self.arrive(yr.at[0:48], 5)
            self.arrive(yr.at[48:96], 6)
            mine = own.at[p.yl, p.z]
            blocks_add(ROWS, [mine, yr], mine)
            for s in range(1, 4):
                self.push(self.piece(mine, lax.rem(p.x + s, 4)), xr.at[s - 1], 6 + s, p.x_peer(s))
        elif n == 5:
            for s in range(1, 4):
                self.arrive(xr.at[s - 1], 6 + s)
            blocks_add(48, [self.piece(own.at[p.yl, p.z], p.x), xr.at[0], xr.at[1], xr.at[2]], xs)
            self.push(xs, hr, 10, p.pair)
        elif n == 6:
            self.arrive(hr, 10)
            mine = self.piece(fin, p.x)
            blocks_add(48, [xs, hr], mine)
            for s in range(1, 4):
                self.push(mine, mine, 10 + s, p.x_peer(s))
        else:
            for s in range(1, 4):
                self.arrive(self.piece(fin, lax.rem(p.x + 4 - s, 4)), 10 + s)
            for cols, out in self.b["out"](k):
                blocks_add(ROWS, [fin.at[:, cols]], out)

    def drain_sib(self):
        if self.sib_sent is not None:
            self.sib_sent.wait_send()
            self.sib_sent = None

    def drain(self):
        self.drain_sib()
        for copy in self.sent:
            copy.wait_send()
        self.sent = []


class ReduceSmall:
    def __init__(self, at, part, b, send, recv):
        self.p, self.part, self.b, self.send, self.recv = at, part, b, send, recv
        self.sent = []

    def push(self, src, dst, sem, peer):
        copy = remote(src, dst, self.send.at[sem], self.recv.at[sem], peer)
        copy.start()
        self.sent.append(copy)

    def arrive(self, ref, sem):
        remote(ref, ref, self.send.at[sem], self.recv.at[sem], self.p.sib).wait_recv()

    def step(self, n):
        p, b = self.p, self.b
        own, sibr, za, zb, yr, dr, out = (b[name] for name in ("own", "sib", "za", "zb", "yr", "dr", "out"))
        if n == 0:
            self.push(self.part.at[:, :, 1 - p.c], sibr, 0, p.sib)
        elif n == 1:
            self.arrive(sibr, 0)
            for yl in range(2):
                for z in range(4):
                    own[yl, z] = self.part[yl, z, p.c] + sibr[yl, z]
            self.push(own.at[:, p.z2, 0:24], za.at[0], 1, p.fore)
            self.push(own.at[:, p.z2, 24:48], za.at[1], 2, p.back)
        elif n == 2:
            self.arrive(za.at[0], 1)
            self.arrive(za.at[1], 2)
            for yl in range(2):
                own[yl, p.zp, 0:24] = own[yl, p.zp, 0:24] + za[0, yl]
                own[yl, p.zm, 24:48] = own[yl, p.zm, 24:48] + za[1, yl]
            self.push(own.at[:, p.zp], zb.at[0], 3, p.fore)
            self.push(own.at[:, p.zm], zb.at[1], 4, p.back)
        elif n == 3:
            self.arrive(zb.at[0], 3)
            self.arrive(zb.at[1], 4)
            for yl in range(2):
                own[yl, p.z] = own[yl, p.z] + zb[0, yl] + zb[1, yl]
            theirs = own.at[1 - p.yl, p.z]
            self.push(theirs.at[0:24], yr.at[0:24], 5, p.up)
            self.push(theirs.at[24:48], yr.at[24:48], 6, p.down)
        elif n == 4:
            self.arrive(yr.at[0:24], 5)
            self.arrive(yr.at[24:48], 6)
            dr[p.dp] = own[p.yl, p.z] + yr[...]
            for s in range(1, 8):
                self.push(dr.at[p.dp], dr.at[p.dp], 6 + s, p.dp_peer(s))
        elif n == 5:
            for s in range(1, 8):
                self.arrive(dr.at[lax.rem(p.dp + 8 - s, 8)], 6 + s)
            total = dr[0]
            for s in range(1, 8):
                total = total + dr[s]
            out[...] = total

    def drain(self):
        for copy in self.sent:
            copy.wait_send()


def dot(a, b, dims=((1,), (0,))):
    return lax.dot_general(a, b, (dims, ((), ())), preferred_element_type=f32)


def lanes(start, size=128):
    return pl.ds(pl.multiple_of(start, 128), size)


def rows8(start, size):
    return pl.ds(pl.multiple_of(start, 8), size)


class Block:
    def __init__(self, b):
        self.b = b
        self.pad_rows = HALF * U

    def turn(self, to_frames):
        i = lax.broadcasted_iota(jnp.int32, (N, N), 0)
        k = lax.broadcasted_iota(jnp.int32, (N, N), 1)
        if not to_frames:
            i, k = k, i
        source = (i & (U - 1)) * L + lax.shift_right_logical(i, 3)
        return (k == source).astype(f32).astype(bf16)

    def setup(self):
        b = self.b
        b["turn"][...] = self.turn(True)
        b["back"][...] = self.turn(False)
        zero = jnp.zeros((self.pad_rows, TILE), f32)
        for name in ("gpad", "cpad"):
            b[name][0 : self.pad_rows] = zero
            b[name][self.pad_rows + N :] = zero
        b["rows"][...] = jnp.zeros((40, D), f32)

    def table(self):
        b = self.b
        for j in range(16):
            b["tab"][:, ROWS * j : ROWS * (j + 1)] = b["small"][j][0:40, 0:ROWS]

    def liveness(self):
        b = self.b
        limit = jnp.concatenate([b["lens"][u, 0:1, :] for u in range(U)], axis=0)

        @pl.loop(0, L)
        def _(l):
            b["live"][rows8(l * U, U), :] = (limit > l).astype(f32)

    def turn_in(self, name):
        ref, turn = self.b[name], self.b["turn"][...]
        for c in range(0, D, JOBW):
            ref[:, c : c + JOBW] = dot(turn, ref[:, c : c + JOBW]).astype(bf16)

    def norm(self):
        b = self.b

        @pl.loop(0, N // 32)
        def _(k):
            r = rows8(k * 32, 32)
            x = b["x"][r, :].astype(f32)
            mean = jnp.sum(x, axis=1, keepdims=True) * (1.0 / D)
            x = x - mean
            inverse = lax.rsqrt(jnp.sum(x * x, axis=1, keepdims=True) * (1.0 / D) + EPS)
            b["mean"][r, :] = jnp.broadcast_to(mean, (32, 128))
            b["inv"][r, :] = jnp.broadcast_to(inverse, (32, 128))
            b["normed"][r, :] = (x * inverse * b["tab"][31:32, :]).astype(bf16)

    def mask(self):
        b = self.b

        @pl.loop(0, N // 32)
        def _(k):
            r = rows8(k * 32, 32)
            b["masked"][r, :] = (b["g"][r, :].astype(f32) * b["live"][r, 0:1]).astype(bf16)

    def glu(self, t):
        b = self.b
        for part in range(2):
            for h in range(2):
                r = slice(h * 256, (h + 1) * 256)
                out = dot(b["normed"][r, :], b["w"][t, :, part * TILE : (part + 1) * TILE])
                if part == 0:
                    b["a"][r, t * TILE : (t + 1) * TILE] = out
                else:
                    b["sig"][r, t * TILE : (t + 1) * TILE] = jax.nn.sigmoid(out)
        self.fill_glu(t)

    def fill_glu(self, t):
        b = self.b

        @pl.loop(0, N // 32)
        def _(k):
            r = rows8(k * 32, 32)
            live = b["live"][r, 0:1]
            cols = slice(t * TILE, (t + 1) * TILE)
            value = (b["a"][r, cols] * b["sig"][r, cols] * live).astype(bf16).astype(f32)
            b["gpad"][rows8(self.pad_rows + k * 32, 32), :] = value

    def taps(self, ref, base, local, wide, flip):
        b = self.b
        window = [ref[rows8(base + 8 * i, 8), local] for i in range(8)]
        sums = [jnp.zeros((8, 128), f32)] * 8
        for t in range(TAPS):
            row = TAPS - 1 - t if flip else t
            tap = jnp.broadcast_to(b["tab"][row : row + 1, wide], (8, 128))
            sums = [s + tap * v for s, v in zip(sums, window)]
            if t < TAPS - 1:
                window = window[1:] + [ref[rows8(base + 8 * (8 + t), 8), local]]
        return jnp.concatenate(sums, axis=0)

    def conv(self, t):
        b = self.b

        @pl.loop(0, 3 * 8)
        def _(n):
            g, base = n // 8, lax.rem(n, 8) * 64
            local, wide = lanes(g * 128), lanes(t * TILE + g * 128)
            out = self.taps(b["gpad"], base, local, wide, False) + b["tab"][32:33, wide]
            sig = jax.nn.sigmoid(out)
            r = rows8(base, 64)
            b["swished"][r, wide] = (out * sig).astype(bf16)
            b["slope"][r, wide] = sig * (1.0 + out * (1.0 - sig))

    def encode(self, h, flush):
        b = self.b
        cols = slice(h * JOBW, (h + 1) * JOBW)
        for q in range(2):
            r = slice(q * 256, (q + 1) * 256)
            out = dot(b["swished"][r, :], b["p"][h])
            b["masked"][r, 0:JOBW] = (b["x"][r, cols].astype(f32) + out * b["live"][r, 0:1]).astype(bf16)
        for q in range(2):
            r = slice(q * 256, (q + 1) * 256)
            b["masked"][r, JOBW:D] = dot(b["back"][r, :], b["masked"][:, 0:JOBW]).astype(bf16)
        flush(h)

    def put(self, job, m, out, cols):
        mix = self.b["mix"]
        for q in range(4):
            j = 4 * m + q
            mix[job.slot(j % 2), j // 8, (j % 8) // 2, :, cols] = out[q * ROWS : (q + 1) * ROWS].astype(bf16)

    def project_part(self, h, job):
        b = self.b
        for m in range(4):
            out = dot(b["swished"][:, m * TILE : (m + 1) * TILE], b["masked"][:, h * JOBW : (h + 1) * JOBW], ((0,), (0,)))
            self.put(job, m, out, slice(0, JOBW))

    def back_project(self, t):
        b = self.b
        cols = slice(t * TILE, (t + 1) * TILE)
        for q in range(2):
            r = slice(q * 256, (q + 1) * 256)
            out = dot(b["masked"][r, 0:JOBW], b["p"][0, cols, :], ((1,), (1,)))
            out = out + dot(b["masked"][r, JOBW:D], b["p"][1, cols, :], ((1,), (1,)))
            b["slope"][r, cols] = out * b["slope"][r, cols]

    def tap_grads(self, t):
        b = self.b
        self.fill_glu(t)

        @pl.loop(0, N // 32)
        def _(k):
            b["cpad"][rows8(self.pad_rows + k * 32, 32), :] = b["slope"][rows8(k * 32, 32), t * TILE : (t + 1) * TILE]

        @pl.loop(0, 3)
        def _(g):
            local, wide = lanes(g * 128), lanes(t * TILE + g * 128)
            for first, count in ((0, 16), (16, 15)):

                def step(n, sums):
                    base = n * 64
                    ups = [b["cpad"][rows8(self.pad_rows + base + 8 * i, 8), local] for i in range(8)]
                    window = [b["gpad"][rows8(base + 8 * (first + i), 8), local] for i in range(count)]
                    for i in range(8):
                        sums = [s + ups[i] * v for s, v in zip(sums[:count], window)] + sums[count:]
                        if i < 7:
                            window = window[1:] + [b["gpad"][rows8(base + 8 * (first + count + i), 8), local]]
                    if first:
                        sums = sums[:count] + [sums[count] + ((ups[0] + ups[1]) + (ups[2] + ups[3])) + ((ups[4] + ups[5]) + (ups[6] + ups[7]))]
                    return sums

                extra = 1 if first else 0
                sums = lax.fori_loop(0, 8, step, [jnp.zeros((8, 128), f32)] * (count + extra))
                for i in range(count):
                    b["rows"][first + i : first + i + 1, wide] = jnp.sum(sums[i], axis=0, keepdims=True)
                if first:
                    b["rows"][32:33, wide] = jnp.sum(sums[count], axis=0, keepdims=True)

    def back_conv(self, t):
        b = self.b

        @pl.loop(0, 3 * 8)
        def _(n):
            g, base = n // 8, lax.rem(n, 8) * 64
            local, wide = lanes(g * 128), lanes(t * TILE + g * 128)
            r = rows8(base, 64)
            grad = self.taps(b["cpad"], base, local, wide, True) * b["live"][r, :]
            sig = b["sig"][r, wide]
            grad = grad * sig
            b["ge"][t, r, local] = grad.astype(bf16)
            b["ge"][t, r, lanes(TILE + g * 128)] = (grad * b["a"][r, wide] * (1.0 - sig)).astype(bf16)

    def expand_part(self, t, job):
        b = self.b
        for m in range(4):
            out = dot(b["normed"][:, m * TILE : (m + 1) * TILE], b["ge"][t], ((0,), (0,)))
            self.put(job, m, out, slice(0, JOBW))

    def norm_back(self, q):
        b = self.b
        r = slice(q * 128, (q + 1) * 128)
        out = dot(b["ge"][0, r, :], b["w"][0], ((1,), (1,)))
        for t in range(1, TILES):
            out = out + dot(b["ge"][t, r, :], b["w"][t], ((1,), (1,)))
        b["gn"][...] = out

        @pl.loop(0, 8)
        def _(k):
            r = rows8(q * 128 + k * 16, 16)
            gn = b["gn"][rows8(k * 16, 16), :]
            inverse = b["inv"][r, 0:1]
            standard = (b["x"][r, :].astype(f32) - b["mean"][r, 0:1]) * inverse
            both = gn * standard
            b["gain8"][...] += both[0:8] + both[8:16]
            gain = b["tab"][31:32, :]
            h = gn * gain
            m1 = jnp.sum(h, axis=1, keepdims=True) * (1.0 / D)
            m2 = jnp.sum(both * gain, axis=1, keepdims=True) * (1.0 / D)
            grad = inverse * (h - m1 - standard * m2)
            b["normed"][r, :] = (b["g"][r, :].astype(f32) + grad).astype(bf16)

    def turn_out(self):
        b = self.b
        for c in range(0, D, JOBW):
            b["normed"][:, c : c + JOBW] = dot(b["back"][...], b["normed"][:, c : c + JOBW]).astype(bf16)


VMEM_NAMES = (
    ("x", (N, D), bf16), ("g", (N, D), bf16), ("lens", (U, 8, 128), jnp.int32), ("small", (16, 48, 128), f32),
    ("w", (TILES, D, JOBW), bf16), ("p", (2, D, JOBW), bf16),
    ("masked", (N, D), bf16), ("normed", (N, D), bf16), ("a", (N, D), f32), ("sig", (N, D), f32),
    ("slope", (N, D), f32), ("swished", (N, D), bf16), ("ge", (TILES, N, JOBW), bf16),
    ("gpad", (N + 2 * HALF * U, TILE), f32), ("cpad", (N + 2 * HALF * U, TILE), f32),
    ("live", (N, 128), f32), ("mean", (N, 128), f32), ("inv", (N, 128), f32),
    ("turn", (N, N), bf16), ("back", (N, N), bf16), ("tab", (40, D), f32), ("rows", (40, D), f32),
    ("gain8", (8, D), f32), ("gn", (128, D), f32),
    ("mix", (OWN_RING + SEND_RING, 2, 4, ROWS, JOBW), bf16), ("sib", (JOBS, 2, 4, ROWS, JOBW), bf16),
    ("za", (JOBS, 2, 2, 48, JOBW), bf16), ("zb", (JOBS, 2, 2, ROWS, JOBW), bf16), ("yr", (JOBS, ROWS, JOBW), bf16),
    ("xr", (JOBS, 3, 48, 384), bf16), ("xs", (JOBS, 48, 384), bf16), ("hr", (JOBS, 48, 384), bf16),
    ("fin", (JOBS, ROWS, JOBW), bf16),
    ("spart", (2, 4, 2, 48, 128), f32), ("sown", (2, 4, 48, 128), f32), ("ssib", (2, 4, 48, 128), f32),
    ("sza", (2, 2, 24, 128), f32), ("szb", (2, 2, 48, 128), f32), ("syr", (48, 128), f32), ("sdr", (8, 48, 128), f32),
)
SEMS = (
    ("xs_", (4, 8)), ("xr_", (4, 8)), ("gs_", (7, 18)), ("gr_", (7, 18)), ("rs_", (JOBS, 14)), ("rr_", (JOBS, 14)),
    ("ss_", (14,)), ("sr_", (14,)), ("fill_", (12,)), ("enc_", (2,)),
)


def whole_kernel(frames, cot, lens, small, expand, project, o_enc, o_grad, o_small, o_expand, o_project, *scratch):
    b = dict(zip([n[0] for n in VMEM_NAMES + SEMS], scratch))
    at = Place()
    mine = pl.ds(pl.multiple_of(at.sh * ROWS, ROWS), ROWS)
    moves = [(small, b["small"].at[at.sh])]
    for t in range(TILES):
        for part in range(2):
            moves.append((expand.at[:, pl.ds(part * D + t * TILE, TILE)], b["w"].at[t, mine, pl.ds(part * TILE, TILE)]))
    for h in range(2):
        moves.append((project.at[:, pl.ds(h * JOBW, JOBW)], b["p"].at[h, mine, :]))
    fills = [pltpu.make_async_copy(s, d, b["fill_"].at[k]) for k, (s, d) in enumerate(moves)]
    for fill in fills:
        fill.start()
    at.greet()

    def slots(ref):
        return lambda q: ref.at[pl.ds(pl.multiple_of(q * L, L), L), :]

    def sems(k):
        return b["xs_"].at[k], b["xr_"].at[k]

    ex_len = Exchange(at, lambda q: lens.at[q], lambda q: b["lens"].at[q], *sems(0))
    for fill in fills:
        fill.wait()

    def block_small(j, start, size):
        return b["small"].at[j, pl.ds(start, size), :]

    def block_of(ref):
        return lambda j, start, size: ref.at[pl.ds(pl.multiple_of(j * ROWS + start, 48), size), :]

    gathers = [Gather(at, block_small, 48, b["gs_"], b["gr_"], 0)]
    for t in range(TILES):
        gathers.append(Gather(at, block_of(b["w"].at[t]), ROWS, b["gs_"], b["gr_"], 1 + t))
    for h in range(2):
        gathers.append(Gather(at, block_of(b["p"].at[h]), ROWS, b["gs_"], b["gr_"], 5 + h))
    for gather in gathers:
        gather.first()
    ex_x = Exchange(at, lambda q: frames.at[q], slots(b["x"]), *sems(1))
    begun = [0]

    def gather_wave():
        begun[0] = min(begun[0] + 1, len(gathers))
        for gather in gathers[: begun[0]]:
            gather.advance()

    def gathered(k):
        while gathers[k].done < 6:
            gather_wave()

    block = Block(b)
    gather_wave()
    gather_wave()
    ex_g = Exchange(at, lambda q: cot.at[q], slots(b["g"]), *sems(2))
    block.setup()
    gather_wave()
    ex_len.wait()
    block.liveness()
    gather_wave()
    gathered(0)
    block.table()
    gather_wave()
    ex_x.wait()
    block.turn_in("x")
    gather_wave()
    block.norm()
    for t in range(TILES):
        gathered(1 + t)
        block.glu(t)
        gather_wave()
        block.conv(t)
        if t == 1:
            gather_wave()
            ex_g.wait()
            block.turn_in("g")
            block.mask()
    gathered(5)
    gathered(6)
    ex_x.drain()
    ex_g.drain()
    ex_len.drain()
    for gather in gathers:
        gather.drain()

    def out(k):
        if k < 2:
            return [(slice(0, JOBW), o_project.at[:, k * JOBW : (k + 1) * JOBW])]
        t = k - 2
        return [
            (slice(part * TILE, (part + 1) * TILE), o_expand.at[:, part * D + t * TILE : part * D + (t + 1) * TILE])
            for part in range(2)
        ]

    bufs = {**b, "out": out}
    jobs = []

    def job_for(k):
        job = Reduce(at, k, bufs, (b["rs_"], b["rr_"]))
        if k >= SEND_RING:
            jobs[k - SEND_RING].drain_sib()
        if k >= OWN_RING:
            jobs[k - OWN_RING].drain()
        return job

    def launch(job):
        job.advance()
        jobs.append(job)

    def wave():
        for job in jobs:
            job.advance()

    enc_out = []

    def flush(h):
        copy = pltpu.make_async_copy(b["masked"].at[:, pl.ds(JOBW, JOBW)], o_enc.at[:, pl.ds(h * JOBW, JOBW)], b["enc_"].at[h])
        copy.start()
        enc_out.append(copy)

    for h in range(2):
        job = job_for(h)
        block.project_part(h, job)
        launch(job)
    for t in range(TILES):
        block.back_project(t)
        if t == 1:
            wave()
    wave()
    for t in range(TILES):
        block.tap_grads(t)
        wave()
        block.back_conv(t)
        wave()
        while 2 + t >= OWN_RING and jobs[2 + t - OWN_RING].done < 8:
            wave()
        job = job_for(2 + t)
        block.expand_part(t, job)
        launch(job)
    b["gain8"][...] = jnp.zeros((8, D), f32)
    wave()
    for q in range(4):
        block.norm_back(q)
        wave()
    block.turn_out()
    ex_back = Exchange(at, slots(b["normed"]), lambda q: o_grad.at[q], *sems(3))
    b["rows"][31:32, :] = jnp.sum(b["gain8"][...], axis=0, keepdims=True)
    for j in range(16):
        values = b["rows"][:, ROWS * j : ROWS * (j + 1)].astype(bf16).astype(f32)
        b["spart"][j // 8, (j % 8) // 2, j % 2] = jnp.zeros((48, 128), f32)
        b["spart"][j // 8, (j % 8) // 2, j % 2, 0:40, 0:ROWS] = values
    tiny = ReduceSmall(
        at, b["spart"],
        {"own": b["sown"], "sib": b["ssib"], "za": b["sza"], "zb": b["szb"], "yr": b["syr"], "dr": b["sdr"], "out": o_small},
        b["ss_"], b["sr_"],
    )
    tiny.step(0)
    wave()
    for h in range(2):
        for copy in enc_out:
            copy.wait()
        block.encode(h, flush)
        wave()
        tiny.step(1 + h)
    enc_out[-1].wait()
    for n in range(3, 6):
        wave()
        tiny.step(n)
    while any(job.done < 8 for job in jobs):
        wave()
    ex_back.wait()
    ex_back.drain()
    tiny.drain()
    for job in jobs:
        job.drain()


def whole(frames, cot, lens, small, expand, project):
    any_spec = pl.BlockSpec(memory_space=pl.ANY)
    vmem = pl.BlockSpec(memory_space=pltpu.VMEM)
    return pl.pallas_call(
        whole_kernel,
        out_shape=[
            jax.ShapeDtypeStruct((N, D), bf16),
            jax.ShapeDtypeStruct((U, L, D), bf16),
            jax.ShapeDtypeStruct((48, 128), f32),
            jax.ShapeDtypeStruct((ROWS, 2 * D), f32),
            jax.ShapeDtypeStruct((ROWS, D), f32),
        ],
        in_specs=[any_spec] * 6,
        out_specs=[any_spec, any_spec, vmem, vmem, vmem],
        scratch_shapes=[pltpu.VMEM(s, d) for _, s, d in VMEM_NAMES] + [pltpu.SemaphoreType.DMA(s) for _, s in SEMS],
        compiler_params=pltpu.CompilerParams(
            collective_id=0, has_side_effects=True, vmem_limit_bytes=64 * 1024 * 1024 - 64 * 1024
        ),
    )(frames, cot, lens, small, expand, project)


def body(frames, cotangent, lengths, send_order, norm_gain, conv_bias, kernel, expand_weight, project_weight):
    count, length, width = frames.shape
    staged_frames = frames.at[send_order].get(mode="promise_in_bounds")
    staged_cot = cotangent.at[send_order].get(mode="promise_in_bounds")
    staged_len = jnp.broadcast_to(lengths.at[send_order].get(mode="promise_in_bounds")[:, None, None], (U, 8, 128))
    small = jnp.concatenate([kernel.T, norm_gain[None], conv_bias[None]], axis=0).astype(f32)
    small = jnp.pad(small, ((0, 48 - 33), (0, 128 - ROWS)))
    encoded, returned, g_small, g_expand, g_project = whole(
        staged_frames, staged_cot, staged_len, small, expand_weight, project_weight
    )
    plan = (send_order[None, :] == lax.broadcasted_iota(jnp.int32, (count, count), 0)).astype(bf16)
    frame_grad = jnp.einsum("kp,pfh->kfh", plan, returned, preferred_element_type=f32).astype(bf16)
    return (
        encoded.reshape(count, length, width), frame_grad,
        g_small[31, :ROWS], g_small[32, :ROWS], g_small[:31, :ROWS].T, g_expand, g_project,
    )


def solution(mesh):
    both, shard = P(("dp", "shard"), None, None), P("shard", None)
    return jax.shard_map(
        body,
        mesh=mesh,
        in_specs=(both, both, P(("dp", "shard")), P(("dp", "shard")), P("shard"), P("shard"), shard, shard, shard),
        out_specs=(both, both, P("shard"), P("shard"), shard, shard, shard),
        check_vma=False,
    )
```

```python
import jax
import jax.numpy as jnp
from jax import lax
from jax.experimental import pallas as pl
from jax.experimental.pallas import tpu as pltpu
from jax.sharding import PartitionSpec as P

EPS = 1e-05
MESH = pl.DeviceIdType.MESH
D, L, U, ROWS = 1536, 64, 8, 96
JOBW, JOBS, TILE, TILES, TAPS, HALF, SPAN = 768, 6, 384, 4, 31, 15, 16
N = U * L
f32, bf16 = jnp.float32, jnp.bfloat16


class Place:
    def __init__(self):
        self.dp, self.sh = lax.axis_index("dp"), lax.axis_index("shard")
        self.x, self.yh = self.dp // 2, lax.rem(self.dp, 2)
        self.yl = self.sh // 8
        self.z = lax.rem(self.sh, 8) // 2
        self.c = lax.rem(self.sh, 2)
        self.zp, self.zm, self.z2 = (lax.rem(self.z + k, 4) for k in (1, 3, 2))
        y = self.yh * 2 + self.yl
        other = 1 - self.yl

        def at_y(step):
            return (self.x * 2 + lax.rem(y + step, 4) // 2, other * 8 + self.z * 2 + self.c)

        self.up, self.down = at_y(1), at_y(3)
        self.fore = (self.dp, self.yl * 8 + self.zp * 2 + self.c)
        self.back = (self.dp, self.yl * 8 + self.zm * 2 + self.c)
        self.sib = (self.dp, self.yl * 8 + self.z * 2 + 1 - self.c)
        self.pair = (self.x * 2 + 1 - self.yh, self.sh)

    def dp_peer(self, step):
        return (lax.rem(self.dp + step, 8), self.sh)

    def z_peer(self, step):
        return (self.dp, self.yl * 8 + lax.rem(self.z + step, 4) * 2 + self.c)

    def x_peer(self, step):
        return (lax.rem(self.x + step, 4) * 2 + self.yh, self.sh)

    def shard_of(self, yl, z, c):
        return yl * 8 + z * 2 + c

    def greet(self):
        barrier = pltpu.get_barrier_semaphore()
        peers = [self.up, self.down, self.fore, self.back, self.z_peer(2), self.sib] + [self.dp_peer(k) for k in range(1, 8)]
        for peer in peers:
            pl.semaphore_signal(barrier, inc=1, device_id=peer, device_id_type=MESH)
        pl.semaphore_wait(barrier, len(peers))


def remote(src, dst, send, recv, peer):
    return pltpu.make_async_remote_copy(
        src_ref=src, dst_ref=dst, send_sem=send, recv_sem=recv, device_id=peer, device_id_type=MESH
    )


class Gather:
    def __init__(self, at, block, rows, send, recv, job):
        self.p, self.block, self.rows = at, block, rows
        self.s, self.r = (lambda k: send.at[job, k]), (lambda k: recv.at[job, k])
        self.a, self.b, self.full = (0, rows // 2), (rows // 2, rows // 2), (0, rows)
        self.sent, self.done = [], 0

    def push(self, shard, part, sem, peer):
        ref = self.block(shard, *part)
        copy = remote(ref, ref, self.s(sem), self.r(sem), peer)
        copy.start()
        self.sent.append(copy)

    def arrive(self, shard, part, sem):
        ref = self.block(shard, *part)
        remote(ref, ref, self.s(sem), self.r(sem), self.p.sib).wait_recv()

    def first(self):
        self.push(self.p.sh, self.a, 0, self.p.up)
        self.push(self.p.sh, self.b, 1, self.p.down)

    def advance(self):
        if self.done < 6:
            self.step(self.done)
            self.done += 1

    def step(self, n):
        p = self.p
        own, opp = p.yl, 1 - p.yl
        if n == 0:
            self.push(p.sh, self.full, 2, p.fore)
            self.push(p.sh, self.full, 3, p.back)
            self.push(p.sh, self.full, 10, p.sib)
        elif n == 1:
            j = p.shard_of(opp, p.z, p.c)
            self.arrive(j, self.a, 0)
            self.arrive(j, self.b, 1)
            self.push(j, self.full, 4, p.fore)
            self.push(j, self.full, 5, p.back)
            self.push(j, self.full, 11, p.sib)
        elif n in (2, 3):
            yl, k, f, s = (own, 2, 6, 12) if n == 2 else (opp, 4, 8, 14)
            m, q = p.shard_of(yl, p.zm, p.c), p.shard_of(yl, p.zp, p.c)
            self.arrive(m, self.full, k)
            self.push(m, self.a, f, p.fore)
            self.push(m, self.full, s, p.sib)
            self.arrive(q, self.full, k + 1)
            self.push(q, self.b, f + 1, p.back)
            self.push(q, self.full, s + 1, p.sib)
        elif n == 4:
            for yl, k, s in ((own, 6, 16), (opp, 8, 17)):
                j = p.shard_of(yl, p.z2, p.c)
                self.arrive(j, self.a, k)
                self.arrive(j, self.b, k + 1)
                self.push(j, self.full, s, p.sib)
        else:
            d = 1 - p.c
            order = (
                (own, p.z), (opp, p.z), (own, p.zm), (own, p.zp), (opp, p.zm), (opp, p.zp), (own, p.z2), (opp, p.z2),
            )
            for k, (yl, z) in enumerate(order):
                self.arrive(p.shard_of(yl, z, d), self.full, 10 + k)

    def drain(self):
        for copy in self.sent:
            copy.wait_send()


class Exchange:
    def __init__(self, at, src, dst, send, recv):
        self.p, self.src, self.dst, self.s, self.r, self.sent = at, src, dst, send, recv, []
        for k in range(1, 8):
            peer = at.dp_peer(k)
            copy = remote(src(peer[0]), dst(at.dp), send.at[k], recv.at[k], peer)
            copy.start()
            self.sent.append(copy)
        self.own = pltpu.make_async_copy(src(at.dp), dst(at.dp), send.at[0])
        self.own.start()

    def wait(self):
        self.own.wait()
        for k in range(1, 8):
            slot = lax.rem(self.p.dp + 8 - k, 8)
            remote(self.src(slot), self.dst(slot), self.s.at[k], self.r.at[k], self.p.sib).wait_recv()

    def drain(self):
        for copy in self.sent:
            copy.wait_send()


def blocks_add(rows, pieces, out):
    step = 16

    @pl.loop(0, rows // step)
    def _(k):
        span = pl.ds(pl.multiple_of(k * step, step), step)
        total = pieces[0][span, :].astype(f32)
        for piece in pieces[1:]:
            total = total + piece[span, :].astype(f32)
        out[span, :] = total.astype(out.dtype)


def pairs_add(rows, pieces, out):
    step = 16

    @pl.loop(0, rows // step)
    def _(k):
        span = pl.ds(pl.multiple_of(k * step, step), step)
        a, b, c, d = (piece[span, :].astype(f32) for piece in pieces)
        out[span, :] = ((a + b) + (c + d)).astype(out.dtype)


OWN_RING, SEND_RING = 6, 2
EXPAND_JOBS, PROJECT_JOBS = (0, 1, 4, 5), (2, 3)
FIRST = ("y", "x", "y", "z", "y", "y")
KIND_AT = tuple(FIRST[:k].count(f) for k, f in enumerate(FIRST))


class Reduce:
    def __init__(self, at, job, b, sems):
        self.p, self.job, self.b = at, job, b
        self.send, self.recv = sems
        self.sent, self.sib_sent, self.done = [], None, 0
        self.own_at, self.send_at = job % OWN_RING, OWN_RING + job % SEND_RING

    def slot(self, core):
        return self.own_at + lax.rem(core + self.p.c, 2) * (self.send_at - self.own_at)

    def push(self, src, dst, sem, peer):
        copy = remote(src, dst, self.send.at[self.job, sem], self.recv.at[self.job, sem], peer)
        copy.start()
        self.sent.append(copy)

    def arrive(self, ref, sem):
        remote(ref, ref, self.send.at[self.job, sem], self.recv.at[self.job, sem], self.p.sib).wait_recv()

    def quarter(self, ref, q):
        rows, cols = pl.ds((q // 2) * 48, 48), pl.ds(pl.multiple_of(lax.rem(q, 2) * 384, 128), 384)
        return ref.at[(slice(None),) * (len(ref.shape) - 2) + (rows, cols)]

    @property
    def last(self):
        return 7 if FIRST[self.job] == "y" else 6

    def advance(self):
        if self.done < self.last:
            if FIRST[self.job] == "y" and 0 < self.done < self.last - 1:
                self.step_y(self.done)
            else:
                self.step(min(self.done, 5) if self.done < 5 else 5 if self.done == self.last - 1 else self.done)
            self.done += 1

    def core_sum(self):
        own, sibr = self.b["mix"].at[self.own_at], self.b["sib"].at[self.job]
        self.arrive(sibr, 0)
        for yl in range(2):
            for z in range(4):
                blocks_add(ROWS, [own.at[yl, z], sibr.at[yl, z]], own.at[yl, z])
        return own

    def step_y(self, n):
        p, k = self.p, self.job
        yh, zr, xr, pr = (self.b[m].at[KIND_AT[k]] for m in ("yhalf", "zr", "xr", "pr"))
        own, fin = self.b["mix"].at[self.own_at], self.b["fin"].at[k]
        mine = own.at[p.yl, p.z]
        if n == 1:
            self.core_sum()
            theirs = own.at[1 - p.yl]
            self.push(theirs.at[:, 0:48], yh.at[:, 0:48], 1, p.up)
            self.push(theirs.at[:, 48:96], yh.at[:, 48:96], 2, p.down)
        elif n == 2:
            self.arrive(yh.at[:, 0:48], 1)
            self.arrive(yh.at[:, 48:96], 2)
            for s in (1, 2, 3, 0):
                z = lax.rem(p.z + s, 4)
                blocks_add(ROWS, [own.at[p.yl, z], yh.at[z]], own.at[p.yl, z])
                if s:
                    self.push(own.at[p.yl, z], zr.at[s - 1], 2 + s, p.z_peer(s))
        elif n == 3:
            for s in range(1, 4):
                self.arrive(zr.at[s - 1], 2 + s)
            blocks_add(ROWS, [mine] + [zr.at[s] for s in range(3)], mine)
            for s in range(1, 4):
                self.push(self.quarter(mine, lax.rem(p.x + s, 4)), xr.at[s - 1], 5 + s, p.x_peer(s))
        elif n == 4:
            for s in range(1, 4):
                self.arrive(xr.at[s - 1], 5 + s)
            here = self.quarter(mine, p.x)
            blocks_add(48, [here] + [xr.at[s] for s in range(3)], here)
            self.push(here, pr, 9, p.pair)
        else:
            self.arrive(pr, 9)
            here = self.quarter(fin, p.x)
            blocks_add(48, [self.quarter(mine, p.x), pr], here)
            for s in range(1, 4):
                self.push(here, here, 9 + s, p.x_peer(s))

    def step(self, n):
        p, k = self.p, self.job
        fin = self.b["fin"].at[k]
        if n == 0:
            self.push(self.b["mix"].at[self.send_at], self.b["sib"].at[k], 0, p.sib)
            self.sib_sent = self.sent.pop()
            return
        if n == 5:
            for s in range(1, 4):
                self.arrive(self.quarter(fin, lax.rem(p.x + 4 - s, 4)), 9 + s)
            for cols, out in self.b["out"](k):
                blocks_add(ROWS, [fin.at[:, cols]], out)
            return
        two, yr = (self.b[m].at[KIND_AT[k] + (FIRST[k] == "z") * FIRST.count("x")] for m in ("two", "yr"))
        one = self.b["onex" if FIRST[k] == "x" else "onez"].at[KIND_AT[k]]
        own = self.b["mix"].at[self.own_at]
        over_x = FIRST[k] == "x"
        if n == 1:
            self.core_sum()
            for s in range(1, 4):
                if over_x:
                    self.push(self.quarter(own, lax.rem(p.x + s, 4)), one.at[s - 1], s, p.x_peer(s))
                else:
                    self.push(own.at[:, lax.rem(p.z + s, 4)], one.at[s - 1], s, p.z_peer(s))
        elif n == 2:
            for s in range(1, 4):
                self.arrive(one.at[s - 1], s)
            for yl in range(2):
                if over_x:
                    for z in range(4):
                        mine = self.quarter(own.at[yl, z], p.x)
                        blocks_add(48, [mine] + [one.at[s, yl, z] for s in range(3)], mine)
                else:
                    mine = own.at[yl, p.z]
                    blocks_add(ROWS, [mine] + [one.at[s, yl] for s in range(3)], mine)
            for s in range(1, 4):
                if over_x:
                    self.push(self.quarter(own.at[:, lax.rem(p.z + s, 4)], p.x), two.at[s - 1], 3 + s, p.z_peer(s))
                else:
                    self.push(self.quarter(own.at[:, p.z], lax.rem(p.x + s, 4)), two.at[s - 1], 3 + s, p.x_peer(s))
        elif n == 3:
            for s in range(1, 4):
                self.arrive(two.at[s - 1], 3 + s)
            for yl in range(2):
                mine = self.quarter(own.at[yl, p.z], p.x)
                blocks_add(48, [mine] + [two.at[s, yl] for s in range(3)], mine)
            theirs = self.quarter(own.at[1 - p.yl, p.z], p.x)
            self.push(theirs, yr.at[0], 7, p.up)
            self.push(theirs, yr.at[1], 8, p.down)
            self.push(self.quarter(own.at[p.yl, p.z], p.x), yr.at[2], 9, p.pair)
        elif n == 4:
            for s in range(3):
                self.arrive(yr.at[s], 7 + s)
            here = self.quarter(fin, p.x)
            pairs_add(48, [self.quarter(own.at[p.yl, p.z], p.x), yr.at[2], yr.at[0], yr.at[1]], here)
            for s in range(1, 4):
                self.push(here, here, 9 + s, p.x_peer(s))

    def drain_sib(self):
        if self.sib_sent is not None:
            self.sib_sent.wait_send()
            self.sib_sent = None

    def drain(self):
        self.drain_sib()
        for copy in self.sent:
            copy.wait_send()
        self.sent = []


class ReduceSmall:
    def __init__(self, at, part, b, send, recv):
        self.p, self.part, self.b, self.send, self.recv = at, part, b, send, recv
        self.sent = []

    def push(self, src, dst, sem, peer):
        copy = remote(src, dst, self.send.at[sem], self.recv.at[sem], peer)
        copy.start()
        self.sent.append(copy)

    def arrive(self, ref, sem):
        remote(ref, ref, self.send.at[sem], self.recv.at[sem], self.p.sib).wait_recv()

    def step(self, n):
        p, b = self.p, self.b
        own, sibr, za, zb, yr, dr, out = (b[name] for name in ("own", "sib", "za", "zb", "yr", "dr", "out"))
        if n == 0:
            self.push(self.part.at[:, :, 1 - p.c], sibr, 0, p.sib)
        elif n == 1:
            self.arrive(sibr, 0)
            for yl in range(2):
                for z in range(4):
                    own[yl, z] = self.part[yl, z, p.c] + sibr[yl, z]
            self.push(own.at[:, p.z2, 0:24], za.at[0], 1, p.fore)
            self.push(own.at[:, p.z2, 24:48], za.at[1], 2, p.back)
        elif n == 2:
            self.arrive(za.at[0], 1)
            self.arrive(za.at[1], 2)
            for yl in range(2):
                own[yl, p.zp, 0:24] = own[yl, p.zp, 0:24] + za[0, yl]
                own[yl, p.zm, 24:48] = own[yl, p.zm, 24:48] + za[1, yl]
            self.push(own.at[:, p.zp], zb.at[0], 3, p.fore)
            self.push(own.at[:, p.zm], zb.at[1], 4, p.back)
        elif n == 3:
            self.arrive(zb.at[0], 3)
            self.arrive(zb.at[1], 4)
            for yl in range(2):
                own[yl, p.z] = own[yl, p.z] + zb[0, yl] + zb[1, yl]
            theirs = own.at[1 - p.yl, p.z]
            self.push(theirs.at[0:24], yr.at[0:24], 5, p.up)
            self.push(theirs.at[24:48], yr.at[24:48], 6, p.down)
        elif n == 4:
            self.arrive(yr.at[0:24], 5)
            self.arrive(yr.at[24:48], 6)
            dr[p.dp] = own[p.yl, p.z] + yr[...]
            for s in range(1, 8):
                self.push(dr.at[p.dp], dr.at[p.dp], 6 + s, p.dp_peer(s))
        elif n == 5:
            for s in range(1, 8):
                self.arrive(dr.at[lax.rem(p.dp + 8 - s, 8)], 6 + s)
            total = dr[0]
            for s in range(1, 8):
                total = total + dr[s]
            out[...] = total

    def drain(self):
        for copy in self.sent:
            copy.wait_send()


def sigmoid(v):
    return 0.5 * jnp.tanh(0.5 * v) + 0.5


def dot(a, b, dims=((1,), (0,))):
    return lax.dot_general(a, b, (dims, ((), ())), preferred_element_type=f32)


def lanes(start, size=128):
    return pl.ds(pl.multiple_of(start, 128), size)


def rows8(start, size):
    return pl.ds(pl.multiple_of(start, 8), size)


class Block:
    def __init__(self, b):
        self.b = b
        self.pad_rows = HALF * U

    def turn(self, to_frames):
        i = lax.broadcasted_iota(jnp.int32, (N, N), 0)
        k = lax.broadcasted_iota(jnp.int32, (N, N), 1)
        if not to_frames:
            i, k = k, i
        source = (i & (U - 1)) * L + lax.shift_right_logical(i, 3)
        return (k == source).astype(f32).astype(bf16)

    def setup(self):
        b = self.b
        b["turn"][...] = self.turn(True)
        b["back"][...] = self.turn(False)
        zero = jnp.zeros((self.pad_rows, TILE), f32)
        for ref in (b["gpad"].at[0], b["gpad"].at[1], b["cpad"]):
            ref[0 : self.pad_rows] = zero
            ref[self.pad_rows + N :] = zero
        b["rows"][...] = jnp.zeros((40, D), f32)

    def table(self):
        b = self.b
        for j in range(16):
            b["tab"][:, ROWS * j : ROWS * (j + 1)] = b["small"][j][0:40, 0:ROWS]

    def liveness(self):
        b = self.b
        limit = jnp.concatenate([b["lens"][u, 0:1, :] for u in range(U)], axis=0)

        @pl.loop(0, L)
        def _(l):
            b["live"][rows8(l * U, U), :] = (limit > l).astype(f32)

    def turn_in(self, name):
        ref, turn = self.b[name], self.b["turn"][...]
        for c in range(0, D, JOBW):
            ref[:, c : c + JOBW] = dot(turn, ref[:, c : c + JOBW]).astype(bf16)

    def norm(self):
        b = self.b

        @pl.loop(0, N // 32)
        def _(k):
            r = rows8(k * 32, 32)
            x = b["x"][r, :].astype(f32)
            mean = jnp.sum(x, axis=1, keepdims=True) * (1.0 / D)
            x = x - mean
            inverse = lax.rsqrt(jnp.sum(x * x, axis=1, keepdims=True) * (1.0 / D) + EPS)
            b["mean"][r, :] = jnp.broadcast_to(mean, (32, 128))
            b["inv"][r, :] = jnp.broadcast_to(inverse, (32, 128))
            b["normed"][r, :] = (x * inverse * b["tab"][31:32, :]).astype(bf16)

    def mask(self):
        b = self.b

        @pl.loop(0, N // 32)
        def _(k):
            r = rows8(k * 32, 32)
            b["masked"][r, :] = (b["g"][r, :].astype(f32) * b["live"][r, 0:1]).astype(bf16)

    def glu(self, t):
        b = self.b
        for q in range(2):
            r = slice(q * 256, (q + 1) * 256)
            out = dot(b["normed"][r, :], b["w"][t])
            for g in range(3):
                cols = slice(g * 128, (g + 1) * 128)
                value, sig = out[:, cols], sigmoid(out[:, TILE + g * 128 : TILE + (g + 1) * 128])
                b["a"][r, t * TILE + g * 128 : t * TILE + (g + 1) * 128] = value
                b["sig"][t % 2, r, cols] = sig
                live = (value * sig * b["live"][r, :]).astype(bf16).astype(f32)
                b["gpad"][t % 2, self.pad_rows + q * 256 : self.pad_rows + (q + 1) * 256, cols] = live

    def taps(self, ref, base, local, wide, flip):
        b = self.b
        window = [ref[rows8(base + 8 * i, 8), local] for i in range(SPAN)]
        sums = [jnp.zeros((8, 128), f32)] * SPAN
        for t in range(TAPS):
            row = TAPS - 1 - t if flip else t
            tap = jnp.broadcast_to(b["tab"][row : row + 1, wide], (8, 128))
            sums = [s + tap * v for s, v in zip(sums, window)]
            if t < TAPS - 1:
                window = window[1:] + [ref[rows8(base + 8 * (SPAN + t), 8), local]]
        return jnp.concatenate(sums, axis=0)

    def conv(self, t):
        b = self.b

        @pl.loop(0, 3 * (L // SPAN))
        def _(n):
            g, base = n // (L // SPAN), lax.rem(n, L // SPAN) * (SPAN * U)
            local, wide = lanes(g * 128), lanes(t * TILE + g * 128)
            out = self.taps(b["gpad"].at[t % 2], base, local, wide, False) + b["tab"][32:33, wide]
            sig = sigmoid(out)
            r = rows8(base, SPAN * U)
            b["swished"][r, wide] = (out * sig).astype(bf16)
            b["slope"][t % 2, r, local] = sig * (1.0 + out * (1.0 - sig))

    def encode(self, h, flush):
        b = self.b
        cols = slice(h * JOBW, (h + 1) * JOBW)
        for q in range(2):
            r = slice(q * 256, (q + 1) * 256)
            out = dot(b["swished"][r, :], b["p"][h])
            b["masked"][r, 0:JOBW] = (b["x"][r, cols].astype(f32) + out * b["live"][r, 0:1]).astype(bf16)
        for q in range(2):
            r = slice(q * 256, (q + 1) * 256)
            b["masked"][r, JOBW:D] = dot(b["back"][r, :], b["masked"][:, 0:JOBW]).astype(bf16)
        flush(h)

    def put(self, job, m, out, cols):
        mix = self.b["mix"]
        for q in range(4):
            j = 4 * m + q
            mix[job.slot(j % 2), j // 8, (j % 8) // 2, :, cols] = out[q * ROWS : (q + 1) * ROWS].astype(bf16)

    def project_part(self, h, job):
        b = self.b
        for m in range(4):
            out = dot(b["swished"][:, m * TILE : (m + 1) * TILE], b["masked"][:, h * JOBW : (h + 1) * JOBW], ((0,), (0,)))
            self.put(job, m, out, slice(0, JOBW))

    def back_project(self, t):
        b = self.b
        cols = slice(t * TILE, (t + 1) * TILE)
        for q in range(2):
            r = slice(q * 256, (q + 1) * 256)
            out = dot(b["masked"][r, 0:JOBW], b["p"][0, cols, :], ((1,), (1,)))
            out = out + dot(b["masked"][r, JOBW:D], b["p"][1, cols, :], ((1,), (1,)))
            b["cpad"][self.pad_rows + q * 256 : self.pad_rows + (q + 1) * 256, :] = out * b["slope"][t % 2, r, :]

    def tap_grads(self, t):
        b = self.b

        @pl.loop(0, 3)
        def _(g):
            local, wide = lanes(g * 128), lanes(t * TILE + g * 128)
            for first, count in ((0, 16), (16, 15)):

                def step(n, sums):
                    base = n * 64
                    ups = [b["cpad"][rows8(self.pad_rows + base + 8 * i, 8), local] for i in range(8)]
                    window = [b["gpad"][t % 2, rows8(base + 8 * (first + i), 8), local] for i in range(count)]
                    for i in range(8):
                        sums = [s + ups[i] * v for s, v in zip(sums[:count], window)] + sums[count:]
                        if i < 7:
                            window = window[1:] + [b["gpad"][t % 2, rows8(base + 8 * (first + count + i), 8), local]]
                    if first:
                        sums = sums[:count] + [sums[count] + ((ups[0] + ups[1]) + (ups[2] + ups[3])) + ((ups[4] + ups[5]) + (ups[6] + ups[7]))]
                    return sums

                extra = 1 if first else 0
                sums = lax.fori_loop(0, 8, step, [jnp.zeros((8, 128), f32)] * (count + extra))
                for i in range(count):
                    b["rows"][first + i : first + i + 1, wide] = jnp.sum(sums[i], axis=0, keepdims=True)
                if first:
                    b["rows"][32:33, wide] = jnp.sum(sums[count], axis=0, keepdims=True)

    def back_conv(self, t):
        b = self.b

        @pl.loop(0, 3 * (L // SPAN))
        def _(n):
            g, base = n // (L // SPAN), lax.rem(n, L // SPAN) * (SPAN * U)
            local, wide = lanes(g * 128), lanes(t * TILE + g * 128)
            r = rows8(base, SPAN * U)
            grad = self.taps(b["cpad"], base, local, wide, True) * b["live"][r, :]
            sig = b["sig"][t % 2, r, local]
            grad = grad * sig
            b["ge"][t, r, local] = grad.astype(bf16)
            b["ge"][t, r, lanes(TILE + g * 128)] = (grad * b["a"][r, wide] * (1.0 - sig)).astype(bf16)

    def expand_part(self, t, job):
        b = self.b
        for m in range(4):
            out = dot(b["normed"][:, m * TILE : (m + 1) * TILE], b["ge"][t], ((0,), (0,)))
            self.put(job, m, out, slice(0, JOBW))

    def grad_normed(self):
        b = self.b
        for q in range(2):
            r = slice(q * 256, (q + 1) * 256)
            for c in range(2):
                cols = slice(c * JOBW, (c + 1) * JOBW)
                out = dot(b["ge"][0, r, :], b["w"][0, cols, :], ((1,), (1,)))
                for t in range(1, TILES):
                    out = out + dot(b["ge"][t, r, :], b["w"][t, cols, :], ((1,), (1,)))
                b["a"][r, cols] = out

    def norm_back(self, q):
        b = self.b

        @pl.loop(0, 8)
        def _(k):
            r = rows8(q * 128 + k * 16, 16)
            gn = b["a"][r, :]
            inverse = b["inv"][r, 0:1]
            standard = (b["x"][r, :].astype(f32) - b["mean"][r, 0:1]) * inverse
            both = gn * standard
            b["gain8"][...] += both[0:8] + both[8:16]
            gain = b["tab"][31:32, :]
            h = gn * gain
            m1 = jnp.sum(h, axis=1, keepdims=True) * (1.0 / D)
            m2 = jnp.sum(both * gain, axis=1, keepdims=True) * (1.0 / D)
            grad = inverse * (h - m1 - standard * m2)
            b["normed"][r, :] = (b["g"][r, :].astype(f32) + grad).astype(bf16)

    def turn_out(self):
        b = self.b
        for c in range(0, D, JOBW):
            b["normed"][:, c : c + JOBW] = dot(b["back"][...], b["normed"][:, c : c + JOBW]).astype(bf16)


VMEM_NAMES = (
    ("x", (N, D), bf16), ("g", (N, D), bf16), ("lens", (U, 8, 128), jnp.int32), ("small", (16, 48, 128), f32),
    ("w", (TILES, D, JOBW), bf16), ("p", (2, D, JOBW), bf16),
    ("masked", (N, D), bf16), ("normed", (N, D), bf16), ("a", (N, D), f32), ("sig", (2, N, TILE), f32),
    ("slope", (2, N, TILE), f32), ("swished", (N, D), bf16), ("ge", (TILES, N, JOBW), bf16),
    ("gpad", (2, N + 2 * HALF * U, TILE), f32), ("cpad", (N + 2 * HALF * U, TILE), f32),
    ("live", (N, 128), f32), ("mean", (N, 128), f32), ("inv", (N, 128), f32),
    ("turn", (N, N), bf16), ("back", (N, N), bf16), ("tab", (40, D), f32), ("rows", (40, D), f32),
    ("gain8", (8, D), f32),
    ("mix", (OWN_RING + SEND_RING, 2, 4, ROWS, JOBW), bf16), ("sib", (JOBS, 2, 4, ROWS, JOBW), bf16),
    ("onex", (max(1, FIRST.count("x")), 3, 2, 4, 48, 384), bf16), ("onez", (max(1, FIRST.count("z")), 3, 2, ROWS, JOBW), bf16),
    ("two", (2, 3, 2, 48, 384), bf16), ("yr", (2, 3, 48, 384), bf16),
    ("yhalf", (max(1, FIRST.count("y")), 4, ROWS, JOBW), bf16), ("zr", (max(1, FIRST.count("y")), 3, ROWS, JOBW), bf16),
    ("xr", (max(1, FIRST.count("y")), 3, 48, 384), bf16), ("pr", (max(1, FIRST.count("y")), 48, 384), bf16),
    ("fin", (JOBS, ROWS, JOBW), bf16),
    ("spart", (2, 4, 2, 48, 128), f32), ("sown", (2, 4, 48, 128), f32), ("ssib", (2, 4, 48, 128), f32),
    ("sza", (2, 2, 24, 128), f32), ("szb", (2, 2, 48, 128), f32), ("syr", (48, 128), f32), ("sdr", (8, 48, 128), f32),
)
SEMS = (
    ("xs_", (4, 8)), ("xr_", (4, 8)), ("gs_", (7, 18)), ("gr_", (7, 18)), ("rs_", (JOBS, 14)), ("rr_", (JOBS, 14)),
    ("ss_", (14,)), ("sr_", (14,)), ("fill_", (12,)), ("enc_", (2,)),
)


def whole_kernel(frames, cot, lens, small, expand, project, o_enc, o_grad, o_small, o_expand, o_project, *scratch):
    b = dict(zip([n[0] for n in VMEM_NAMES + SEMS], scratch))
    at = Place()
    mine = pl.ds(pl.multiple_of(at.sh * ROWS, ROWS), ROWS)
    moves = [(small, b["small"].at[at.sh])]
    for t in range(TILES):
        for part in range(2):
            moves.append((expand.at[:, pl.ds(part * D + t * TILE, TILE)], b["w"].at[t, mine, pl.ds(part * TILE, TILE)]))
    for h in range(2):
        moves.append((project.at[:, pl.ds(h * JOBW, JOBW)], b["p"].at[h, mine, :]))
    fills = [pltpu.make_async_copy(s, d, b["fill_"].at[k]) for k, (s, d) in enumerate(moves)]
    for fill in fills:
        fill.start()
    at.greet()

    def slots(ref):
        return lambda q: ref.at[pl.ds(pl.multiple_of(q * L, L), L), :]

    def sems(k):
        return b["xs_"].at[k], b["xr_"].at[k]

    ex_len = Exchange(at, lambda q: lens.at[q], lambda q: b["lens"].at[q], *sems(0))
    for fill in fills:
        fill.wait()

    def block_small(j, start, size):
        return b["small"].at[j, pl.ds(start, size), :]

    def block_of(ref):
        return lambda j, start, size: ref.at[pl.ds(pl.multiple_of(j * ROWS + start, 48), size), :]

    gathers = [Gather(at, block_small, 48, b["gs_"], b["gr_"], 0)]
    order = (b["w"].at[0], b["w"].at[1], b["p"].at[0], b["p"].at[1], b["w"].at[2], b["w"].at[3])
    for k, ref in enumerate(order):
        gathers.append(Gather(at, block_of(ref), ROWS, b["gs_"], b["gr_"], 1 + k))
    for gather in gathers:
        gather.first()
    ex_x = Exchange(at, lambda q: frames.at[q], slots(b["x"]), *sems(1))
    clock = [0]
    begins = (0, 0, 2, 4, 6, 8, 10)

    def gather_wave():
        for gather, begin in zip(gathers, begins):
            if clock[0] >= begin:
                gather.advance()
        clock[0] += 1

    def gathered(k):
        while gathers[k].done < 6:
            gather_wave()

    block = Block(b)
    gather_wave()
    ex_g = Exchange(at, lambda q: cot.at[q], slots(b["g"]), *sems(2))
    gather_wave()
    block.setup()
    gather_wave()
    ex_len.wait()
    block.liveness()
    gather_wave()
    gather_wave()
    gathered(0)
    block.table()
    ex_x.wait()
    gather_wave()
    block.turn_in("x")
    gather_wave()
    block.norm()
    gather_wave()

    def out(k):
        if k in PROJECT_JOBS:
            h = PROJECT_JOBS.index(k)
            return [(slice(0, JOBW), o_project.at[:, h * JOBW : (h + 1) * JOBW])]
        t = EXPAND_JOBS.index(k)
        return [
            (slice(part * TILE, (part + 1) * TILE), o_expand.at[:, part * D + t * TILE : part * D + (t + 1) * TILE])
            for part in range(2)
        ]

    bufs = {**b, "out": out}
    jobs = []

    def job_for(k):
        job = Reduce(at, k, bufs, (b["rs_"], b["rr_"]))
        if k >= SEND_RING:
            jobs[k - SEND_RING].drain_sib()
        if k >= OWN_RING:
            jobs[k - OWN_RING].drain()
        return job

    def launch(job):
        job.advance()
        jobs.append(job)

    def wave():
        for job in reversed(jobs):
            job.advance()

    enc_out = []

    def flush(h):
        copy = pltpu.make_async_copy(b["masked"].at[:, pl.ds(JOBW, JOBW)], o_enc.at[:, pl.ds(h * JOBW, JOBW)], b["enc_"].at[h])
        copy.start()
        enc_out.append(copy)

    def forward(t):
        gathered((1, 2, 5, 6)[t])
        block.glu(t)
        gather_wave()
        block.conv(t)
        gather_wave()

    def backward(t):
        block.back_project(t)
        gather_wave()
        block.tap_grads(t)
        gather_wave()
        wave()
        block.back_conv(t)
        gather_wave()
        job = job_for(EXPAND_JOBS[t])
        block.expand_part(t, job)
        launch(job)

    forward(0)
    forward(1)
    ex_g.wait()
    block.turn_in("g")
    gathered(3)
    block.mask()
    gathered(4)
    backward(0)
    forward(2)
    backward(1)
    forward(3)
    for h in range(2):
        job = job_for(PROJECT_JOBS[h])
        block.project_part(h, job)
        launch(job)
    backward(2)
    backward(3)
    ex_x.drain()
    ex_g.drain()
    ex_len.drain()
    for gather in gathers:
        gather.drain()
    b["gain8"][...] = jnp.zeros((8, D), f32)
    block.grad_normed()
    wave()
    for q in range(4):
        block.norm_back(q)
        if q % 2:
            wave()
    block.turn_out()
    ex_back = Exchange(at, slots(b["normed"]), lambda q: o_grad.at[q], *sems(3))
    b["rows"][31:32, :] = jnp.sum(b["gain8"][...], axis=0, keepdims=True)
    for j in range(16):
        values = b["rows"][:, ROWS * j : ROWS * (j + 1)].astype(bf16).astype(f32)
        b["spart"][j // 8, (j % 8) // 2, j % 2] = jnp.zeros((48, 128), f32)
        b["spart"][j // 8, (j % 8) // 2, j % 2, 0:40, 0:ROWS] = values
    tiny = ReduceSmall(
        at, b["spart"],
        {"own": b["sown"], "sib": b["ssib"], "za": b["sza"], "zb": b["szb"], "yr": b["syr"], "dr": b["sdr"], "out": o_small},
        b["ss_"], b["sr_"],
    )
    tiny.step(0)
    wave()
    for h in range(2):
        for copy in enc_out:
            copy.wait()
        block.encode(h, flush)
        wave()
        tiny.step(1 + h)
    enc_out[-1].wait()
    for n in range(3, 6):
        wave()
        tiny.step(n)
    while any(job.done < job.last for job in jobs):
        wave()
    ex_back.wait()
    ex_back.drain()
    tiny.drain()
    for job in jobs:
        job.drain()


def whole(frames, cot, lens, small, expand, project):
    any_spec = pl.BlockSpec(memory_space=pl.ANY)
    vmem = pl.BlockSpec(memory_space=pltpu.VMEM)
    return pl.pallas_call(
        whole_kernel,
        out_shape=[
            jax.ShapeDtypeStruct((N, D), bf16),
            jax.ShapeDtypeStruct((U, L, D), bf16),
            jax.ShapeDtypeStruct((48, 128), f32),
            jax.ShapeDtypeStruct((ROWS, 2 * D), f32),
            jax.ShapeDtypeStruct((ROWS, D), f32),
        ],
        in_specs=[any_spec] * 6,
        out_specs=[any_spec, any_spec, vmem, vmem, vmem],
        scratch_shapes=[pltpu.VMEM(s, d) for _, s, d in VMEM_NAMES] + [pltpu.SemaphoreType.DMA(s) for _, s in SEMS],
        compiler_params=pltpu.CompilerParams(
            collective_id=0, has_side_effects=True, vmem_limit_bytes=64 * 1024 * 1024 - 64 * 1024
        ),
    )(frames, cot, lens, small, expand, project)


def body(frames, cotangent, lengths, send_order, norm_gain, conv_bias, kernel, expand_weight, project_weight):
    count, length, width = frames.shape
    staged_frames = frames.at[send_order].get(mode="promise_in_bounds")
    staged_cot = cotangent.at[send_order].get(mode="promise_in_bounds")
    staged_len = jnp.broadcast_to(lengths.at[send_order].get(mode="promise_in_bounds")[:, None, None], (U, 8, 128))
    small = jnp.concatenate([kernel.T, norm_gain[None], conv_bias[None]], axis=0).astype(f32)
    small = jnp.pad(small, ((0, 48 - 33), (0, 128 - ROWS)))
    encoded, returned, g_small, g_expand, g_project = whole(
        staged_frames, staged_cot, staged_len, small, expand_weight, project_weight
    )
    plan = (send_order[None, :] == lax.broadcasted_iota(jnp.int32, (count, count), 0)).astype(bf16)
    frame_grad = jnp.einsum("kp,pfh->kfh", plan, returned, preferred_element_type=f32).astype(bf16)
    return (
        encoded.reshape(count, length, width), frame_grad,
        g_small[31, :ROWS], g_small[32, :ROWS], g_small[:31, :ROWS].T, g_expand, g_project,
    )


def solution(mesh):
    both, shard = P(("dp", "shard"), None, None), P("shard", None)
    return jax.shard_map(
        body,
        mesh=mesh,
        in_specs=(both, both, P(("dp", "shard")), P(("dp", "shard")), P("shard"), P("shard"), shard, shard, shard),
        out_specs=(both, both, P("shard"), P("shard"), shard, shard, shard),
        check_vma=False,
    )
```

```python
import jax
import jax.numpy as jnp
from jax import lax
from jax.experimental import pallas as pl
from jax.experimental.pallas import tpu as pltpu
from jax.sharding import PartitionSpec as P

EPS = 1e-05
MESH = pl.DeviceIdType.MESH
D, L, U, ROWS = 1536, 64, 8, 96
JOBW, JOBS, TILE, TILES, TAPS, HALF, SPAN = 768, 6, 384, 4, 31, 15, 16
N = U * L
f32, bf16 = jnp.float32, jnp.bfloat16


class Place:
    def __init__(self):
        self.dp, self.sh = lax.axis_index("dp"), lax.axis_index("shard")
        self.x, self.yh = self.dp // 2, lax.rem(self.dp, 2)
        self.yl = self.sh // 8
        self.z = lax.rem(self.sh, 8) // 2
        self.c = lax.rem(self.sh, 2)
        self.zp, self.zm, self.z2 = (lax.rem(self.z + k, 4) for k in (1, 3, 2))
        y = self.yh * 2 + self.yl
        other = 1 - self.yl

        def at_y(step):
            return (self.x * 2 + lax.rem(y + step, 4) // 2, other * 8 + self.z * 2 + self.c)

        self.up, self.down = at_y(1), at_y(3)
        self.fore = (self.dp, self.yl * 8 + self.zp * 2 + self.c)
        self.back = (self.dp, self.yl * 8 + self.zm * 2 + self.c)
        self.sib = (self.dp, self.yl * 8 + self.z * 2 + 1 - self.c)
        self.pair = (self.x * 2 + 1 - self.yh, self.sh)

    def dp_peer(self, step):
        return (lax.rem(self.dp + step, 8), self.sh)

    def z_peer(self, step):
        return (self.dp, self.yl * 8 + lax.rem(self.z + step, 4) * 2 + self.c)

    def x_peer(self, step):
        return (lax.rem(self.x + step, 4) * 2 + self.yh, self.sh)

    def shard_of(self, yl, z, c):
        return yl * 8 + z * 2 + c

    def greet(self):
        barrier = pltpu.get_barrier_semaphore()
        peers = [self.up, self.down, self.fore, self.back, self.z_peer(2), self.sib] + [self.dp_peer(k) for k in range(1, 8)]
        for peer in peers:
            pl.semaphore_signal(barrier, inc=1, device_id=peer, device_id_type=MESH)
        pl.semaphore_wait(barrier, len(peers))


def remote(src, dst, send, recv, peer):
    return pltpu.make_async_remote_copy(
        src_ref=src, dst_ref=dst, send_sem=send, recv_sem=recv, device_id=peer, device_id_type=MESH
    )


class Gather:
    def __init__(self, at, block, rows, send, recv, job):
        self.p, self.block, self.rows = at, block, rows
        self.s, self.r = (lambda k: send.at[job, k]), (lambda k: recv.at[job, k])
        self.a, self.b, self.full = (0, rows // 2), (rows // 2, rows // 2), (0, rows)
        self.sent, self.done = [], 0

    def push(self, shard, part, sem, peer):
        ref = self.block(shard, *part)
        copy = remote(ref, ref, self.s(sem), self.r(sem), peer)
        copy.start()
        self.sent.append(copy)

    def arrive(self, shard, part, sem):
        ref = self.block(shard, *part)
        remote(ref, ref, self.s(sem), self.r(sem), self.p.sib).wait_recv()

    def first(self):
        self.push(self.p.sh, self.a, 0, self.p.up)
        self.push(self.p.sh, self.b, 1, self.p.down)

    def advance(self):
        if self.done < 6:
            self.step(self.done)
            self.done += 1

    def step(self, n):
        p = self.p
        own, opp = p.yl, 1 - p.yl
        if n == 0:
            self.push(p.sh, self.full, 2, p.fore)
            self.push(p.sh, self.full, 3, p.back)
            self.push(p.sh, self.full, 10, p.sib)
        elif n == 1:
            j = p.shard_of(opp, p.z, p.c)
            self.arrive(j, self.a, 0)
            self.arrive(j, self.b, 1)
            self.push(j, self.full, 4, p.fore)
            self.push(j, self.full, 5, p.back)
            self.push(j, self.full, 11, p.sib)
        elif n in (2, 3):
            yl, k, f, s = (own, 2, 6, 12) if n == 2 else (opp, 4, 8, 14)
            m, q = p.shard_of(yl, p.zm, p.c), p.shard_of(yl, p.zp, p.c)
            self.arrive(m, self.full, k)
            self.push(m, self.a, f, p.fore)
            self.push(m, self.full, s, p.sib)
            self.arrive(q, self.full, k + 1)
            self.push(q, self.b, f + 1, p.back)
            self.push(q, self.full, s + 1, p.sib)
        elif n == 4:
            for yl, k, s in ((own, 6, 16), (opp, 8, 17)):
                j = p.shard_of(yl, p.z2, p.c)
                self.arrive(j, self.a, k)
                self.arrive(j, self.b, k + 1)
                self.push(j, self.full, s, p.sib)
        else:
            d = 1 - p.c
            order = (
                (own, p.z), (opp, p.z), (own, p.zm), (own, p.zp), (opp, p.zm), (opp, p.zp), (own, p.z2), (opp, p.z2),
            )
            for k, (yl, z) in enumerate(order):
                self.arrive(p.shard_of(yl, z, d), self.full, 10 + k)

    def drain(self):
        for copy in self.sent:
            copy.wait_send()


class Exchange:
    def __init__(self, at, src, dst, send, recv):
        self.p, self.src, self.dst, self.s, self.r, self.sent = at, src, dst, send, recv, []
        for k in range(1, 8):
            peer = at.dp_peer(k)
            copy = remote(src(peer[0]), dst(at.dp), send.at[k], recv.at[k], peer)
            copy.start()
            self.sent.append(copy)
        self.own = pltpu.make_async_copy(src(at.dp), dst(at.dp), send.at[0])
        self.own.start()

    def wait(self):
        self.own.wait()
        for k in range(1, 8):
            slot = lax.rem(self.p.dp + 8 - k, 8)
            remote(self.src(slot), self.dst(slot), self.s.at[k], self.r.at[k], self.p.sib).wait_recv()

    def drain(self):
        for copy in self.sent:
            copy.wait_send()


def blocks_add(rows, pieces, out):
    step = 16

    @pl.loop(0, rows // step)
    def _(k):
        span = pl.ds(pl.multiple_of(k * step, step), step)
        total = pieces[0][span, :].astype(f32)
        for piece in pieces[1:]:
            total = total + piece[span, :].astype(f32)
        out[span, :] = total.astype(out.dtype)


def pairs_add(rows, pieces, out):
    step = 16

    @pl.loop(0, rows // step)
    def _(k):
        span = pl.ds(pl.multiple_of(k * step, step), step)
        a, b, c, d = (piece[span, :].astype(f32) for piece in pieces)
        out[span, :] = ((a + b) + (c + d)).astype(out.dtype)


OWN_RING, SEND_RING = 6, 2
EXPAND_JOBS, PROJECT_JOBS = (0, 1, 4, 5), (2, 3)
FIRST = ("y", "x", "y", "z", "y", "y")
KIND_AT = tuple(FIRST[:k].count(f) for k, f in enumerate(FIRST))


class Reduce:
    def __init__(self, at, job, b, sems):
        self.p, self.job, self.b = at, job, b
        self.send, self.recv = sems
        self.sent, self.sib_sent, self.done = [], None, 0
        self.own_at, self.send_at = job % OWN_RING, OWN_RING + job % SEND_RING

    def slot(self, core):
        return self.own_at + lax.rem(core + self.p.c, 2) * (self.send_at - self.own_at)

    def push(self, src, dst, sem, peer):
        copy = remote(src, dst, self.send.at[self.job, sem], self.recv.at[self.job, sem], peer)
        copy.start()
        self.sent.append(copy)

    def arrive(self, ref, sem):
        remote(ref, ref, self.send.at[self.job, sem], self.recv.at[self.job, sem], self.p.sib).wait_recv()

    def quarter(self, ref, q):
        rows, cols = pl.ds((q // 2) * 48, 48), pl.ds(pl.multiple_of(lax.rem(q, 2) * 384, 128), 384)
        return ref.at[(slice(None),) * (len(ref.shape) - 2) + (rows, cols)]

    @property
    def last(self):
        return 7 if FIRST[self.job] == "y" else 6

    def advance(self):
        if self.done < self.last:
            if FIRST[self.job] == "y" and 0 < self.done < self.last - 1:
                self.step_y(self.done)
            else:
                self.step(min(self.done, 5) if self.done < 5 else 5 if self.done == self.last - 1 else self.done)
            self.done += 1

    def core_sum(self):
        own, sibr = self.b["mix"].at[self.own_at], self.b["sib"].at[self.job]
        self.arrive(sibr, 0)
        for yl in range(2):
            for z in range(4):
                blocks_add(ROWS, [own.at[yl, z], sibr.at[yl, z]], own.at[yl, z])
        return own

    def step_y(self, n):
        p, k = self.p, self.job
        yh, zr, xr, pr = (self.b[m].at[KIND_AT[k]] for m in ("yhalf", "zr", "xr", "pr"))
        own, fin = self.b["mix"].at[self.own_at], self.b["fin"].at[k]
        mine = own.at[p.yl, p.z]
        if n == 1:
            self.core_sum()
            theirs = own.at[1 - p.yl]
            self.push(theirs.at[:, 0:48], yh.at[:, 0:48], 1, p.up)
            self.push(theirs.at[:, 48:96], yh.at[:, 48:96], 2, p.down)
        elif n == 2:
            self.arrive(yh.at[:, 0:48], 1)
            self.arrive(yh.at[:, 48:96], 2)
            for s in (1, 2, 3, 0):
                z = lax.rem(p.z + s, 4)
                blocks_add(ROWS, [own.at[p.yl, z], yh.at[z]], own.at[p.yl, z])
                if s:
                    self.push(own.at[p.yl, z], zr.at[s - 1], 2 + s, p.z_peer(s))
        elif n == 3:
            for s in range(1, 4):
                self.arrive(zr.at[s - 1], 2 + s)
            blocks_add(ROWS, [mine] + [zr.at[s] for s in range(3)], mine)
            for s in range(1, 4):
                self.push(self.quarter(mine, lax.rem(p.x + s, 4)), xr.at[s - 1], 5 + s, p.x_peer(s))
        elif n == 4:
            for s in range(1, 4):
                self.arrive(xr.at[s - 1], 5 + s)
            here = self.quarter(mine, p.x)
            blocks_add(48, [here] + [xr.at[s] for s in range(3)], here)
            self.push(here, pr, 9, p.pair)
        else:
            self.arrive(pr, 9)
            here = self.quarter(fin, p.x)
            blocks_add(48, [self.quarter(mine, p.x), pr], here)
            for s in range(1, 4):
                self.push(here, here, 9 + s, p.x_peer(s))

    def step(self, n):
        p, k = self.p, self.job
        fin = self.b["fin"].at[k]
        if n == 0:
            self.push(self.b["mix"].at[self.send_at], self.b["sib"].at[k], 0, p.sib)
            self.sib_sent = self.sent.pop()
            return
        if n == 5:
            for s in range(1, 4):
                self.arrive(self.quarter(fin, lax.rem(p.x + 4 - s, 4)), 9 + s)
            for cols, out in self.b["out"](k):
                blocks_add(ROWS, [fin.at[:, cols]], out)
            return
        two, yr = (self.b[m].at[KIND_AT[k] + (FIRST[k] == "z") * FIRST.count("x")] for m in ("two", "yr"))
        one = self.b["onex" if FIRST[k] == "x" else "onez"].at[KIND_AT[k]]
        own = self.b["mix"].at[self.own_at]
        over_x = FIRST[k] == "x"
        if n == 1:
            self.core_sum()
            for s in range(1, 4):
                if over_x:
                    self.push(self.quarter(own, lax.rem(p.x + s, 4)), one.at[s - 1], s, p.x_peer(s))
                else:
                    self.push(own.at[:, lax.rem(p.z + s, 4)], one.at[s - 1], s, p.z_peer(s))
        elif n == 2:
            for s in range(1, 4):
                self.arrive(one.at[s - 1], s)
            for yl in range(2):
                if over_x:
                    for z in range(4):
                        mine = self.quarter(own.at[yl, z], p.x)
                        blocks_add(48, [mine] + [one.at[s, yl, z] for s in range(3)], mine)
                else:
                    mine = own.at[yl, p.z]
                    blocks_add(ROWS, [mine] + [one.at[s, yl] for s in range(3)], mine)
            for s in range(1, 4):
                if over_x:
                    self.push(self.quarter(own.at[:, lax.rem(p.z + s, 4)], p.x), two.at[s - 1], 3 + s, p.z_peer(s))
                else:
                    self.push(self.quarter(own.at[:, p.z], lax.rem(p.x + s, 4)), two.at[s - 1], 3 + s, p.x_peer(s))
        elif n == 3:
            for s in range(1, 4):
                self.arrive(two.at[s - 1], 3 + s)
            for yl in range(2):
                mine = self.quarter(own.at[yl, p.z], p.x)
                blocks_add(48, [mine] + [two.at[s, yl] for s in range(3)], mine)
            theirs = self.quarter(own.at[1 - p.yl, p.z], p.x)
            self.push(theirs, yr.at[0], 7, p.up)
            self.push(theirs, yr.at[1], 8, p.down)
            self.push(self.quarter(own.at[p.yl, p.z], p.x), yr.at[2], 9, p.pair)
        elif n == 4:
            for s in range(3):
                self.arrive(yr.at[s], 7 + s)
            here = self.quarter(fin, p.x)
            pairs_add(48, [self.quarter(own.at[p.yl, p.z], p.x), yr.at[2], yr.at[0], yr.at[1]], here)
            for s in range(1, 4):
                self.push(here, here, 9 + s, p.x_peer(s))

    def drain_sib(self):
        if self.sib_sent is not None:
            self.sib_sent.wait_send()
            self.sib_sent = None

    def drain(self):
        self.drain_sib()
        for copy in self.sent:
            copy.wait_send()
        self.sent = []


class ReduceSmall:
    def __init__(self, at, part, b, send, recv):
        self.p, self.part, self.b, self.send, self.recv = at, part, b, send, recv
        self.sent = []

    def push(self, src, dst, sem, peer):
        copy = remote(src, dst, self.send.at[sem], self.recv.at[sem], peer)
        copy.start()
        self.sent.append(copy)

    def arrive(self, ref, sem):
        remote(ref, ref, self.send.at[sem], self.recv.at[sem], self.p.sib).wait_recv()

    def step(self, n):
        p, b = self.p, self.b
        own, sibr, za, zb, yr, dr, out = (b[name] for name in ("own", "sib", "za", "zb", "yr", "dr", "out"))
        if n == 0:
            self.push(self.part.at[:, :, 1 - p.c], sibr, 0, p.sib)
        elif n == 1:
            self.arrive(sibr, 0)
            for yl in range(2):
                for z in range(4):
                    own[yl, z] = self.part[yl, z, p.c] + sibr[yl, z]
            self.push(own.at[:, p.z2, 0:24], za.at[0], 1, p.fore)
            self.push(own.at[:, p.z2, 24:48], za.at[1], 2, p.back)
        elif n == 2:
            self.arrive(za.at[0], 1)
            self.arrive(za.at[1], 2)
            for yl in range(2):
                own[yl, p.zp, 0:24] = own[yl, p.zp, 0:24] + za[0, yl]
                own[yl, p.zm, 24:48] = own[yl, p.zm, 24:48] + za[1, yl]
            self.push(own.at[:, p.zp], zb.at[0], 3, p.fore)
            self.push(own.at[:, p.zm], zb.at[1], 4, p.back)
        elif n == 3:
            self.arrive(zb.at[0], 3)
            self.arrive(zb.at[1], 4)
            for yl in range(2):
                own[yl, p.z] = own[yl, p.z] + zb[0, yl] + zb[1, yl]
            theirs = own.at[1 - p.yl, p.z]
            self.push(theirs.at[0:24], yr.at[0:24], 5, p.up)
            self.push(theirs.at[24:48], yr.at[24:48], 6, p.down)
        elif n == 4:
            self.arrive(yr.at[0:24], 5)
            self.arrive(yr.at[24:48], 6)
            dr[p.dp] = own[p.yl, p.z] + yr[...]
            for s in range(1, 8):
                self.push(dr.at[p.dp], dr.at[p.dp], 6 + s, p.dp_peer(s))
        elif n == 5:
            for s in range(1, 8):
                self.arrive(dr.at[lax.rem(p.dp + 8 - s, 8)], 6 + s)
            total = dr[0]
            for s in range(1, 8):
                total = total + dr[s]
            out[...] = total

    def drain(self):
        for copy in self.sent:
            copy.wait_send()


def sigmoid(v):
    return 0.5 * jnp.tanh(0.5 * v) + 0.5


def dot(a, b, dims=((1,), (0,))):
    return lax.dot_general(a, b, (dims, ((), ())), preferred_element_type=f32)


def lanes(start, size=128):
    return pl.ds(pl.multiple_of(start, 128), size)


def rows8(start, size):
    return pl.ds(pl.multiple_of(start, 8), size)


class Block:
    def __init__(self, b):
        self.b = b
        self.pad_rows = HALF * U

    def turn(self, to_frames):
        i = lax.broadcasted_iota(jnp.int32, (N, N), 0)
        k = lax.broadcasted_iota(jnp.int32, (N, N), 1)
        if not to_frames:
            i, k = k, i
        source = (i & (U - 1)) * L + lax.shift_right_logical(i, 3)
        return (k == source).astype(f32).astype(bf16)

    def setup(self):
        b = self.b
        b["turn"][...] = self.turn(True)
        b["back"][...] = self.turn(False)
        zero = jnp.zeros((self.pad_rows, TILE), f32)
        for ref in (b["gpad"].at[0], b["gpad"].at[1], b["cpad"]):
            ref[0 : self.pad_rows] = zero
            ref[self.pad_rows + N :] = zero
        b["rows"][...] = jnp.zeros((40, D), f32)

    def table(self):
        b = self.b
        for j in range(16):
            b["tab"][:, ROWS * j : ROWS * (j + 1)] = b["small"][j][0:40, 0:ROWS]

    def liveness(self):
        b = self.b
        limit = jnp.concatenate([b["lens"][u, 0:1, :] for u in range(U)], axis=0)

        @pl.loop(0, L)
        def _(l):
            b["live"][rows8(l * U, U), :] = (limit > l).astype(f32)

    def turn_in(self, name):
        ref, turn = self.b[name], self.b["turn"][...]
        for c in range(0, D, JOBW):
            ref[:, c : c + JOBW] = dot(turn, ref[:, c : c + JOBW]).astype(bf16)

    def norm(self):
        b = self.b

        @pl.loop(0, N // 32)
        def _(k):
            r = rows8(k * 32, 32)
            x = b["x"][r, :].astype(f32)
            mean = jnp.sum(x, axis=1, keepdims=True) * (1.0 / D)
            x = x - mean
            inverse = lax.rsqrt(jnp.sum(x * x, axis=1, keepdims=True) * (1.0 / D) + EPS)
            b["mean"][r, :] = jnp.broadcast_to(mean, (32, 128))
            b["inv"][r, :] = jnp.broadcast_to(inverse, (32, 128))
            b["normed"][r, :] = (x * inverse * b["tab"][31:32, :]).astype(bf16)

    def mask(self):
        b = self.b

        @pl.loop(0, N // 32)
        def _(k):
            r = rows8(k * 32, 32)
            b["masked"][r, :] = (b["g"][r, :].astype(f32) * b["live"][r, 0:1]).astype(bf16)

    def glu(self, t):
        b = self.b
        for q in range(2):
            r = slice(q * 256, (q + 1) * 256)
            out = dot(b["normed"][r, :], b["w"][t])
            for g in range(3):
                cols = slice(g * 128, (g + 1) * 128)
                value, sig = out[:, cols], sigmoid(out[:, TILE + g * 128 : TILE + (g + 1) * 128])
                b["a"][r, t * TILE + g * 128 : t * TILE + (g + 1) * 128] = value
                b["sig"][t % 2, r, cols] = sig
                live = (value * sig * b["live"][r, :]).astype(bf16).astype(f32)
                b["gpad"][t % 2, self.pad_rows + q * 256 : self.pad_rows + (q + 1) * 256, cols] = live

    def taps(self, ref, base, local, wide, flip):
        b = self.b
        window = [ref[rows8(base + 8 * i, 8), local] for i in range(SPAN)]
        sums = [jnp.zeros((8, 128), f32)] * SPAN
        for t in range(TAPS):
            row = TAPS - 1 - t if flip else t
            tap = jnp.broadcast_to(b["tab"][row : row + 1, wide], (8, 128))
            sums = [s + tap * v for s, v in zip(sums, window)]
            if t < TAPS - 1:
                window = window[1:] + [ref[rows8(base + 8 * (SPAN + t), 8), local]]
        return jnp.concatenate(sums, axis=0)

    def conv(self, t):
        b = self.b

        @pl.loop(0, 3 * (L // SPAN))
        def _(n):
            g, base = n // (L // SPAN), lax.rem(n, L // SPAN) * (SPAN * U)
            local, wide = lanes(g * 128), lanes(t * TILE + g * 128)
            out = self.taps(b["gpad"].at[t % 2], base, local, wide, False) + b["tab"][32:33, wide]
            sig = sigmoid(out)
            r = rows8(base, SPAN * U)
            b["swished"][r, wide] = (out * sig).astype(bf16)
            b["slope"][t % 2, r, local] = sig * (1.0 + out * (1.0 - sig))

    def encode(self, h, flush):
        b = self.b
        cols = slice(h * JOBW, (h + 1) * JOBW)
        for q in range(2):
            r = slice(q * 256, (q + 1) * 256)
            out = dot(b["swished"][r, :], b["p"][h])
            b["masked"][r, 0:JOBW] = (b["x"][r, cols].astype(f32) + out * b["live"][r, 0:1]).astype(bf16)
        for q in range(2):
            r = slice(q * 256, (q + 1) * 256)
            b["masked"][r, JOBW:D] = dot(b["back"][r, :], b["masked"][:, 0:JOBW]).astype(bf16)
        flush(h)

    def put(self, job, m, out, cols):
        mix = self.b["mix"]
        for q in range(4):
            j = 4 * m + q
            mix[job.slot(j % 2), j // 8, (j % 8) // 2, :, cols] = out[q * ROWS : (q + 1) * ROWS].astype(bf16)

    def project_part(self, h, job):
        b = self.b
        for m in range(4):
            out = dot(b["swished"][:, m * TILE : (m + 1) * TILE], b["masked"][:, h * JOBW : (h + 1) * JOBW], ((0,), (0,)))
            self.put(job, m, out, slice(0, JOBW))

    def back_project(self, t):
        b = self.b
        cols = slice(t * TILE, (t + 1) * TILE)
        for q in range(2):
            r = slice(q * 256, (q + 1) * 256)
            out = dot(b["masked"][r, 0:JOBW], b["p"][0, cols, :], ((1,), (1,)))
            out = out + dot(b["masked"][r, JOBW:D], b["p"][1, cols, :], ((1,), (1,)))
            b["cpad"][self.pad_rows + q * 256 : self.pad_rows + (q + 1) * 256, :] = out * b["slope"][t % 2, r, :]

    def tap_grads(self, t):
        b = self.b

        @pl.loop(0, 3)
        def _(g):
            local, wide = lanes(g * 128), lanes(t * TILE + g * 128)
            for first, count in ((0, 16), (16, 15)):

                def step(n, sums):
                    base = n * 64
                    ups = [b["cpad"][rows8(self.pad_rows + base + 8 * i, 8), local] for i in range(8)]
                    window = [b["gpad"][t % 2, rows8(base + 8 * (first + i), 8), local] for i in range(count)]
                    for i in range(8):
                        sums = [s + ups[i] * v for s, v in zip(sums[:count], window)] + sums[count:]
                        if i < 7:
                            window = window[1:] + [b["gpad"][t % 2, rows8(base + 8 * (first + count + i), 8), local]]
                    if first:
                        sums = sums[:count] + [sums[count] + ((ups[0] + ups[1]) + (ups[2] + ups[3])) + ((ups[4] + ups[5]) + (ups[6] + ups[7]))]
                    return sums

                extra = 1 if first else 0
                sums = lax.fori_loop(0, 8, step, [jnp.zeros((8, 128), f32)] * (count + extra))
                for i in range(count):
                    b["rows"][first + i : first + i + 1, wide] = jnp.sum(sums[i], axis=0, keepdims=True)
                if first:
                    b["rows"][32:33, wide] = jnp.sum(sums[count], axis=0, keepdims=True)

    def back_conv(self, t):
        b = self.b

        @pl.loop(0, 3 * (L // SPAN))
        def _(n):
            g, base = n // (L // SPAN), lax.rem(n, L // SPAN) * (SPAN * U)
            local, wide = lanes(g * 128), lanes(t * TILE + g * 128)
            r = rows8(base, SPAN * U)
            grad = self.taps(b["cpad"], base, local, wide, True) * b["live"][r, :]
            sig = b["sig"][t % 2, r, local]
            grad = grad * sig
            b["ge"][t, r, local] = grad.astype(bf16)
            b["ge"][t, r, lanes(TILE + g * 128)] = (grad * b["a"][r, wide] * (1.0 - sig)).astype(bf16)

    def expand_part(self, t, job):
        b = self.b
        for m in range(4):
            out = dot(b["normed"][:, m * TILE : (m + 1) * TILE], b["ge"][t], ((0,), (0,)))
            self.put(job, m, out, slice(0, JOBW))

    def grad_normed(self):
        b = self.b
        for q in range(2):
            r = slice(q * 256, (q + 1) * 256)
            for c in range(2):
                cols = slice(c * JOBW, (c + 1) * JOBW)
                out = dot(b["ge"][0, r, :], b["w"][0, cols, :], ((1,), (1,)))
                for t in range(1, TILES):
                    out = out + dot(b["ge"][t, r, :], b["w"][t, cols, :], ((1,), (1,)))
                b["a"][r, cols] = out

    def norm_back(self, q):
        b = self.b

        @pl.loop(0, 8)
        def _(k):
            r = rows8(q * 128 + k * 16, 16)
            gn = b["a"][r, :]
            inverse = b["inv"][r, 0:1]
            standard = (b["x"][r, :].astype(f32) - b["mean"][r, 0:1]) * inverse
            both = gn * standard
            b["gain8"][...] += both[0:8] + both[8:16]
            gain = b["tab"][31:32, :]
            h = gn * gain
            m1 = jnp.sum(h, axis=1, keepdims=True) * (1.0 / D)
            m2 = jnp.sum(both * gain, axis=1, keepdims=True) * (1.0 / D)
            grad = inverse * (h - m1 - standard * m2)
            b["normed"][r, :] = (b["g"][r, :].astype(f32) + grad).astype(bf16)

    def turn_out(self):
        b = self.b
        for c in range(0, D, JOBW):
            b["normed"][:, c : c + JOBW] = dot(b["back"][...], b["normed"][:, c : c + JOBW]).astype(bf16)


VMEM_NAMES = (
    ("x", (N, D), bf16), ("g", (N, D), bf16), ("lens", (U, 8, 128), jnp.int32), ("small", (16, 48, 128), f32),
    ("w", (TILES, D, JOBW), bf16), ("p", (2, D, JOBW), bf16),
    ("masked", (N, D), bf16), ("normed", (N, D), bf16), ("a", (N, D), f32), ("sig", (2, N, TILE), f32),
    ("slope", (2, N, TILE), f32), ("swished", (N, D), bf16), ("ge", (TILES, N, JOBW), bf16),
    ("gpad", (2, N + 2 * HALF * U, TILE), f32), ("cpad", (N + 2 * HALF * U, TILE), f32),
    ("live", (N, 128), f32), ("mean", (N, 128), f32), ("inv", (N, 128), f32),
    ("turn", (N, N), bf16), ("back", (N, N), bf16), ("tab", (40, D), f32), ("rows", (40, D), f32),
    ("gain8", (8, D), f32),
    ("mix", (OWN_RING + SEND_RING, 2, 4, ROWS, JOBW), bf16), ("sib", (JOBS, 2, 4, ROWS, JOBW), bf16),
    ("onex", (max(1, FIRST.count("x")), 3, 2, 4, 48, 384), bf16), ("onez", (max(1, FIRST.count("z")), 3, 2, ROWS, JOBW), bf16),
    ("two", (2, 3, 2, 48, 384), bf16), ("yr", (2, 3, 48, 384), bf16),
    ("yhalf", (max(1, FIRST.count("y")), 4, ROWS, JOBW), bf16), ("zr", (max(1, FIRST.count("y")), 3, ROWS, JOBW), bf16),
    ("xr", (max(1, FIRST.count("y")), 3, 48, 384), bf16), ("pr", (max(1, FIRST.count("y")), 48, 384), bf16),
    ("fin", (JOBS, ROWS, JOBW), bf16),
    ("spart", (2, 4, 2, 48, 128), f32), ("sown", (2, 4, 48, 128), f32), ("ssib", (2, 4, 48, 128), f32),
    ("sza", (2, 2, 24, 128), f32), ("szb", (2, 2, 48, 128), f32), ("syr", (48, 128), f32), ("sdr", (8, 48, 128), f32),
)
SEMS = (
    ("xs_", (4, 8)), ("xr_", (4, 8)), ("gs_", (7, 18)), ("gr_", (7, 18)), ("rs_", (JOBS, 14)), ("rr_", (JOBS, 14)),
    ("ss_", (14,)), ("sr_", (14,)), ("fill_", (12,)), ("enc_", (2,)),
)


def whole_kernel(frames, cot, lens, small, expand, project, o_enc, o_grad, o_small, o_expand, o_project, *scratch):
    b = dict(zip([n[0] for n in VMEM_NAMES + SEMS], scratch))
    at = Place()
    mine = pl.ds(pl.multiple_of(at.sh * ROWS, ROWS), ROWS)
    moves = [(small, b["small"].at[at.sh])]
    for t in range(TILES):
        for part in range(2):
            moves.append((expand.at[:, pl.ds(part * D + t * TILE, TILE)], b["w"].at[t, mine, pl.ds(part * TILE, TILE)]))
    for h in range(2):
        moves.append((project.at[:, pl.ds(h * JOBW, JOBW)], b["p"].at[h, mine, :]))
    fills = [pltpu.make_async_copy(s, d, b["fill_"].at[k]) for k, (s, d) in enumerate(moves)]
    for fill in fills:
        fill.start()
    at.greet()

    def slots(ref):
        return lambda q: ref.at[pl.ds(pl.multiple_of(q * L, L), L), :]

    def sems(k):
        return b["xs_"].at[k], b["xr_"].at[k]

    ex_len = Exchange(at, lambda q: lens.at[q], lambda q: b["lens"].at[q], *sems(0))
    for fill in fills:
        fill.wait()

    def block_small(j, start, size):
        return b["small"].at[j, pl.ds(start, size), :]

    def block_of(ref):
        return lambda j, start, size: ref.at[pl.ds(pl.multiple_of(j * ROWS + start, 48), size), :]

    gathers = [Gather(at, block_small, 48, b["gs_"], b["gr_"], 0)]
    order = (b["w"].at[0], b["w"].at[1], b["p"].at[0], b["p"].at[1], b["w"].at[2], b["w"].at[3])
    for k, ref in enumerate(order):
        gathers.append(Gather(at, block_of(ref), ROWS, b["gs_"], b["gr_"], 1 + k))
    for gather in gathers:
        gather.first()
    ex_x = Exchange(at, lambda q: frames.at[q], slots(b["x"]), *sems(1))
    clock = [0]
    begins = (0, 0, 2, 4, 6, 8, 10)

    def gather_wave():
        for gather, begin in zip(gathers, begins):
            if clock[0] >= begin:
                gather.advance()
        clock[0] += 1

    def gathered(k):
        while gathers[k].done < 6:
            gather_wave()

    block = Block(b)
    gather_wave()
    ex_g = Exchange(at, lambda q: cot.at[q], slots(b["g"]), *sems(2))
    gather_wave()
    block.setup()
    gather_wave()
    ex_len.wait()
    block.liveness()
    gather_wave()
    gather_wave()
    gathered(0)
    block.table()
    ex_x.wait()
    gather_wave()
    block.turn_in("x")
    gather_wave()
    block.norm()
    gather_wave()

    def out(k):
        if k in PROJECT_JOBS:
            h = PROJECT_JOBS.index(k)
            return [(slice(0, JOBW), o_project.at[:, h * JOBW : (h + 1) * JOBW])]
        t = EXPAND_JOBS.index(k)
        return [
            (slice(part * TILE, (part + 1) * TILE), o_expand.at[:, part * D + t * TILE : part * D + (t + 1) * TILE])
            for part in range(2)
        ]

    bufs = {**b, "out": out}
    jobs = []

    def job_for(k):
        job = Reduce(at, k, bufs, (b["rs_"], b["rr_"]))
        if k >= SEND_RING:
            jobs[k - SEND_RING].drain_sib()
        if k >= OWN_RING:
            jobs[k - OWN_RING].drain()
        return job

    def launch(job):
        job.advance()
        jobs.append(job)

    def wave():
        for job in reversed(jobs):
            job.advance()

    enc_out = []

    def flush(h):
        copy = pltpu.make_async_copy(b["masked"].at[:, pl.ds(JOBW, JOBW)], o_enc.at[:, pl.ds(h * JOBW, JOBW)], b["enc_"].at[h])
        copy.start()
        enc_out.append(copy)

    def forward(t):
        gathered((1, 2, 5, 6)[t])
        block.glu(t)
        gather_wave()
        block.conv(t)
        gather_wave()

    def backward(t):
        block.back_project(t)
        block.tap_grads(t)
        gather_wave()
        wave()
        block.back_conv(t)
        gather_wave()
        job = job_for(EXPAND_JOBS[t])
        block.expand_part(t, job)
        launch(job)

    forward(0)
    forward(1)
    ex_g.wait()
    block.turn_in("g")
    gathered(3)
    block.mask()
    gathered(4)
    backward(0)
    forward(2)
    backward(1)
    forward(3)
    for h in range(2):
        job = job_for(PROJECT_JOBS[h])
        block.project_part(h, job)
        launch(job)
    backward(2)
    backward(3)
    ex_x.drain()
    ex_g.drain()
    ex_len.drain()
    for gather in gathers:
        gather.drain()
    b["gain8"][...] = jnp.zeros((8, D), f32)
    block.grad_normed()
    wave()
    for q in range(4):
        block.norm_back(q)
    block.turn_out()
    ex_back = Exchange(at, slots(b["normed"]), lambda q: o_grad.at[q], *sems(3))
    b["rows"][31:32, :] = jnp.sum(b["gain8"][...], axis=0, keepdims=True)
    for j in range(16):
        values = b["rows"][:, ROWS * j : ROWS * (j + 1)].astype(bf16).astype(f32)
        b["spart"][j // 8, (j % 8) // 2, j % 2] = jnp.zeros((48, 128), f32)
        b["spart"][j // 8, (j % 8) // 2, j % 2, 0:40, 0:ROWS] = values
    tiny = ReduceSmall(
        at, b["spart"],
        {"own": b["sown"], "sib": b["ssib"], "za": b["sza"], "zb": b["szb"], "yr": b["syr"], "dr": b["sdr"], "out": o_small},
        b["ss_"], b["sr_"],
    )
    tiny.step(0)
    wave()
    for h in range(2):
        for copy in enc_out:
            copy.wait()
        block.encode(h, flush)
        wave()
        tiny.step(1 + h)
    enc_out[-1].wait()
    for n in range(3, 6):
        wave()
        tiny.step(n)
    while any(job.done < job.last for job in jobs):
        wave()
    ex_back.wait()
    ex_back.drain()
    tiny.drain()
    for job in jobs:
        job.drain()


def whole(frames, cot, lens, small, expand, project):
    any_spec = pl.BlockSpec(memory_space=pl.ANY)
    vmem = pl.BlockSpec(memory_space=pltpu.VMEM)
    return pl.pallas_call(
        whole_kernel,
        out_shape=[
            jax.ShapeDtypeStruct((N, D), bf16),
            jax.ShapeDtypeStruct((U, L, D), bf16),
            jax.ShapeDtypeStruct((48, 128), f32),
            jax.ShapeDtypeStruct((ROWS, 2 * D), f32),
            jax.ShapeDtypeStruct((ROWS, D), f32),
        ],
        in_specs=[any_spec] * 6,
        out_specs=[any_spec, any_spec, vmem, vmem, vmem],
        scratch_shapes=[pltpu.VMEM(s, d) for _, s, d in VMEM_NAMES] + [pltpu.SemaphoreType.DMA(s) for _, s in SEMS],
        compiler_params=pltpu.CompilerParams(
            collective_id=0, has_side_effects=True, vmem_limit_bytes=64 * 1024 * 1024 - 64 * 1024
        ),
    )(frames, cot, lens, small, expand, project)


def body(frames, cotangent, lengths, send_order, norm_gain, conv_bias, kernel, expand_weight, project_weight):
    count, length, width = frames.shape
    staged_frames = frames.at[send_order].get(mode="promise_in_bounds")
    staged_cot = cotangent.at[send_order].get(mode="promise_in_bounds")
    staged_len = jnp.broadcast_to(lengths.at[send_order].get(mode="promise_in_bounds")[:, None, None], (U, 8, 128))
    small = jnp.concatenate([kernel.T, norm_gain[None], conv_bias[None]], axis=0).astype(f32)
    small = jnp.pad(small, ((0, 48 - 33), (0, 128 - ROWS)))
    encoded, returned, g_small, g_expand, g_project = whole(
        staged_frames, staged_cot, staged_len, small, expand_weight, project_weight
    )
    plan = (send_order[None, :] == lax.broadcasted_iota(jnp.int32, (count, count), 0)).astype(bf16)
    frame_grad = jnp.einsum("kp,pfh->kfh", plan, returned, preferred_element_type=f32).astype(bf16)
    return (
        encoded.reshape(count, length, width), frame_grad,
        g_small[31, :ROWS], g_small[32, :ROWS], g_small[:31, :ROWS].T, g_expand, g_project,
    )


def solution(mesh):
    both, shard = P(("dp", "shard"), None, None), P("shard", None)
    return jax.shard_map(
        body,
        mesh=mesh,
        in_specs=(both, both, P(("dp", "shard")), P(("dp", "shard")), P("shard"), P("shard"), shard, shard, shard),
        out_specs=(both, both, P("shard"), P("shard"), shard, shard, shard),
        check_vma=False,
    )
```

```python
import jax
import jax.numpy as jnp
from jax import lax
from jax.experimental import pallas as pl
from jax.experimental.pallas import tpu as pltpu
from jax.sharding import PartitionSpec as P

EPS = 1e-05
MESH = pl.DeviceIdType.MESH
D, L, U, ROWS = 1536, 64, 8, 96
JOBW, JOBS, TILE, TILES, TAPS, HALF, SPAN = 768, 6, 384, 4, 31, 15, 16
N = U * L
f32, bf16 = jnp.float32, jnp.bfloat16


class Place:
    def __init__(self):
        self.dp, self.sh = lax.axis_index("dp"), lax.axis_index("shard")
        self.x, self.yh = self.dp // 2, lax.rem(self.dp, 2)
        self.yl = self.sh // 8
        self.z = lax.rem(self.sh, 8) // 2
        self.c = lax.rem(self.sh, 2)
        self.zp, self.zm, self.z2 = (lax.rem(self.z + k, 4) for k in (1, 3, 2))
        y = self.yh * 2 + self.yl
        other = 1 - self.yl

        def at_y(step):
            return (self.x * 2 + lax.rem(y + step, 4) // 2, other * 8 + self.z * 2 + self.c)

        self.up, self.down = at_y(1), at_y(3)
        self.fore = (self.dp, self.yl * 8 + self.zp * 2 + self.c)
        self.back = (self.dp, self.yl * 8 + self.zm * 2 + self.c)
        self.sib = (self.dp, self.yl * 8 + self.z * 2 + 1 - self.c)
        self.pair = (self.x * 2 + 1 - self.yh, self.sh)

    def dp_peer(self, step):
        return (lax.rem(self.dp + step, 8), self.sh)

    def z_peer(self, step):
        return (self.dp, self.yl * 8 + lax.rem(self.z + step, 4) * 2 + self.c)

    def x_peer(self, step):
        return (lax.rem(self.x + step, 4) * 2 + self.yh, self.sh)

    def shard_of(self, yl, z, c):
        return yl * 8 + z * 2 + c

    def greet(self):
        barrier = pltpu.get_barrier_semaphore()
        peers = [self.up, self.down, self.fore, self.back, self.z_peer(2), self.sib] + [self.dp_peer(k) for k in range(1, 8)]
        for peer in peers:
            pl.semaphore_signal(barrier, inc=1, device_id=peer, device_id_type=MESH)
        pl.semaphore_wait(barrier, len(peers))


def remote(src, dst, send, recv, peer):
    return pltpu.make_async_remote_copy(
        src_ref=src, dst_ref=dst, send_sem=send, recv_sem=recv, device_id=peer, device_id_type=MESH
    )


class Gather:
    def __init__(self, at, block, rows, send, recv, job):
        self.p, self.block, self.rows = at, block, rows
        self.s, self.r = (lambda k: send.at[job, k]), (lambda k: recv.at[job, k])
        self.a, self.b, self.full = (0, rows // 2), (rows // 2, rows // 2), (0, rows)
        self.sent, self.done = [], 0

    def push(self, shard, part, sem, peer):
        ref = self.block(shard, *part)
        copy = remote(ref, ref, self.s(sem), self.r(sem), peer)
        copy.start()
        self.sent.append(copy)

    def arrive(self, shard, part, sem):
        ref = self.block(shard, *part)
        remote(ref, ref, self.s(sem), self.r(sem), self.p.sib).wait_recv()

    def first(self):
        self.push(self.p.sh, self.a, 0, self.p.up)
        self.push(self.p.sh, self.b, 1, self.p.down)

    def advance(self):
        if self.done < 6:
            self.step(self.done)
            self.done += 1

    def step(self, n):
        p = self.p
        own, opp = p.yl, 1 - p.yl
        if n == 0:
            self.push(p.sh, self.full, 2, p.fore)
            self.push(p.sh, self.full, 3, p.back)
            self.push(p.sh, self.full, 10, p.sib)
        elif n == 1:
            j = p.shard_of(opp, p.z, p.c)
            self.arrive(j, self.a, 0)
            self.arrive(j, self.b, 1)
            self.push(j, self.full, 4, p.fore)
            self.push(j, self.full, 5, p.back)
            self.push(j, self.full, 11, p.sib)
        elif n in (2, 3):
            yl, k, f, s = (own, 2, 6, 12) if n == 2 else (opp, 4, 8, 14)
            m, q = p.shard_of(yl, p.zm, p.c), p.shard_of(yl, p.zp, p.c)
            self.arrive(m, self.full, k)
            self.push(m, self.a, f, p.fore)
            self.push(m, self.full, s, p.sib)
            self.arrive(q, self.full, k + 1)
            self.push(q, self.b, f + 1, p.back)
            self.push(q, self.full, s + 1, p.sib)
        elif n == 4:
            for yl, k, s in ((own, 6, 16), (opp, 8, 17)):
                j = p.shard_of(yl, p.z2, p.c)
                self.arrive(j, self.a, k)
                self.arrive(j, self.b, k + 1)
                self.push(j, self.full, s, p.sib)
        else:
            d = 1 - p.c
            order = (
                (own, p.z), (opp, p.z), (own, p.zm), (own, p.zp), (opp, p.zm), (opp, p.zp), (own, p.z2), (opp, p.z2),
            )
            for k, (yl, z) in enumerate(order):
                self.arrive(p.shard_of(yl, z, d), self.full, 10 + k)

    def drain(self):
        for copy in self.sent:
            copy.wait_send()


class Exchange:
    def __init__(self, at, src, dst, send, recv):
        self.p, self.src, self.dst, self.s, self.r, self.sent = at, src, dst, send, recv, []
        for k in range(1, 8):
            peer = at.dp_peer(k)
            copy = remote(src(peer[0]), dst(at.dp), send.at[k], recv.at[k], peer)
            copy.start()
            self.sent.append(copy)
        self.own = pltpu.make_async_copy(src(at.dp), dst(at.dp), send.at[0])
        self.own.start()

    def wait(self):
        self.own.wait()
        for k in range(1, 8):
            slot = lax.rem(self.p.dp + 8 - k, 8)
            remote(self.src(slot), self.dst(slot), self.s.at[k], self.r.at[k], self.p.sib).wait_recv()

    def drain(self):
        for copy in self.sent:
            copy.wait_send()


def blocks_add(rows, pieces, out):
    step = 16

    @pl.loop(0, rows // step)
    def _(k):
        span = pl.ds(pl.multiple_of(k * step, step), step)
        total = pieces[0][span, :].astype(f32)
        for piece in pieces[1:]:
            total = total + piece[span, :].astype(f32)
        out[span, :] = total.astype(out.dtype)


def pairs_add(rows, pieces, out):
    step = 16

    @pl.loop(0, rows // step)
    def _(k):
        span = pl.ds(pl.multiple_of(k * step, step), step)
        a, b, c, d = (piece[span, :].astype(f32) for piece in pieces)
        out[span, :] = ((a + b) + (c + d)).astype(out.dtype)


OWN_RING, SEND_RING = 6, 2
EXPAND_JOBS, PROJECT_JOBS = (0, 1, 4, 5), (2, 3)
FIRST = ("y", "x", "y", "z", "y", "y")
KIND_AT = tuple(FIRST[:k].count(f) for k, f in enumerate(FIRST))


class Reduce:
    def __init__(self, at, job, b, sems):
        self.p, self.job, self.b = at, job, b
        self.send, self.recv = sems
        self.sent, self.sib_sent, self.done = [], None, 0
        self.own_at, self.send_at = job % OWN_RING, OWN_RING + job % SEND_RING

    def slot(self, core):
        return self.own_at + lax.rem(core + self.p.c, 2) * (self.send_at - self.own_at)

    def push(self, src, dst, sem, peer):
        copy = remote(src, dst, self.send.at[self.job, sem], self.recv.at[self.job, sem], peer)
        copy.start()
        self.sent.append(copy)

    def arrive(self, ref, sem):
        remote(ref, ref, self.send.at[self.job, sem], self.recv.at[self.job, sem], self.p.sib).wait_recv()

    def quarter(self, ref, q):
        rows, cols = pl.ds((q // 2) * 48, 48), pl.ds(pl.multiple_of(lax.rem(q, 2) * 384, 128), 384)
        return ref.at[(slice(None),) * (len(ref.shape) - 2) + (rows, cols)]

    @property
    def last(self):
        return 7 if FIRST[self.job] == "y" else 6

    def advance(self):
        if self.done < self.last:
            if FIRST[self.job] == "y" and 0 < self.done < self.last - 1:
                self.step_y(self.done)
            else:
                self.step(min(self.done, 5) if self.done < 5 else 5 if self.done == self.last - 1 else self.done)
            self.done += 1

    def core_sum(self):
        own, sibr = self.b["mix"].at[self.own_at], self.b["sib"].at[self.job]
        self.arrive(sibr, 0)
        for yl in range(2):
            for z in range(4):
                blocks_add(ROWS, [own.at[yl, z], sibr.at[yl, z]], own.at[yl, z])
        return own

    def step_y(self, n):
        p, k = self.p, self.job
        yh, zr, xr, pr = (self.b[m].at[KIND_AT[k]] for m in ("yhalf", "zr", "xr", "pr"))
        own, fin = self.b["mix"].at[self.own_at], self.b["fin"].at[k]
        mine = own.at[p.yl, p.z]
        if n == 1:
            self.core_sum()
            theirs = own.at[1 - p.yl]
            self.push(theirs.at[:, 0:48], yh.at[:, 0:48], 1, p.up)
            self.push(theirs.at[:, 48:96], yh.at[:, 48:96], 2, p.down)
        elif n == 2:
            self.arrive(yh.at[:, 0:48], 1)
            self.arrive(yh.at[:, 48:96], 2)
            for s in (1, 2, 3, 0):
                z = lax.rem(p.z + s, 4)
                blocks_add(ROWS, [own.at[p.yl, z], yh.at[z]], own.at[p.yl, z])
                if s:
                    self.push(own.at[p.yl, z], zr.at[s - 1], 2 + s, p.z_peer(s))
        elif n == 3:
            for s in range(1, 4):
                self.arrive(zr.at[s - 1], 2 + s)
            blocks_add(ROWS, [mine] + [zr.at[s] for s in range(3)], mine)
            for s in range(1, 4):
                self.push(self.quarter(mine, lax.rem(p.x + s, 4)), xr.at[s - 1], 5 + s, p.x_peer(s))
        elif n == 4:
            for s in range(1, 4):
                self.arrive(xr.at[s - 1], 5 + s)
            here = self.quarter(mine, p.x)
            blocks_add(48, [here] + [xr.at[s] for s in range(3)], here)
            self.push(here, pr, 9, p.pair)
        else:
            self.arrive(pr, 9)
            here = self.quarter(fin, p.x)
            blocks_add(48, [self.quarter(mine, p.x), pr], here)
            for s in range(1, 4):
                self.push(here, here, 9 + s, p.x_peer(s))

    def step(self, n):
        p, k = self.p, self.job
        fin = self.b["fin"].at[k]
        if n == 0:
            self.push(self.b["mix"].at[self.send_at], self.b["sib"].at[k], 0, p.sib)
            self.sib_sent = self.sent.pop()
            return
        if n == 5:
            for s in range(1, 4):
                self.arrive(self.quarter(fin, lax.rem(p.x + 4 - s, 4)), 9 + s)
            for cols, out in self.b["out"](k):
                blocks_add(ROWS, [fin.at[:, cols]], out)
            return
        two, yr = (self.b[m].at[KIND_AT[k] + (FIRST[k] == "z") * FIRST.count("x")] for m in ("two", "yr"))
        one = self.b["onex" if FIRST[k] == "x" else "onez"].at[KIND_AT[k]]
        own = self.b["mix"].at[self.own_at]
        over_x = FIRST[k] == "x"
        if n == 1:
            self.core_sum()
            for s in range(1, 4):
                if over_x:
                    self.push(self.quarter(own, lax.rem(p.x + s, 4)), one.at[s - 1], s, p.x_peer(s))
                else:
                    self.push(own.at[:, lax.rem(p.z + s, 4)], one.at[s - 1], s, p.z_peer(s))
        elif n == 2:
            for s in range(1, 4):
                self.arrive(one.at[s - 1], s)
            for yl in range(2):
                if over_x:
                    for z in range(4):
                        mine = self.quarter(own.at[yl, z], p.x)
                        blocks_add(48, [mine] + [one.at[s, yl, z] for s in range(3)], mine)
                else:
                    mine = own.at[yl, p.z]
                    blocks_add(ROWS, [mine] + [one.at[s, yl] for s in range(3)], mine)
            for s in range(1, 4):
                if over_x:
                    self.push(self.quarter(own.at[:, lax.rem(p.z + s, 4)], p.x), two.at[s - 1], 3 + s, p.z_peer(s))
                else:
                    self.push(self.quarter(own.at[:, p.z], lax.rem(p.x + s, 4)), two.at[s - 1], 3 + s, p.x_peer(s))
        elif n == 3:
            for s in range(1, 4):
                self.arrive(two.at[s - 1], 3 + s)
            for yl in range(2):
                mine = self.quarter(own.at[yl, p.z], p.x)
                blocks_add(48, [mine] + [two.at[s, yl] for s in range(3)], mine)
            theirs = self.quarter(own.at[1 - p.yl, p.z], p.x)
            self.push(theirs, yr.at[0], 7, p.up)
            self.push(theirs, yr.at[1], 8, p.down)
            self.push(self.quarter(own.at[p.yl, p.z], p.x), yr.at[2], 9, p.pair)
        elif n == 4:
            for s in range(3):
                self.arrive(yr.at[s], 7 + s)
            here = self.quarter(fin, p.x)
            pairs_add(48, [self.quarter(own.at[p.yl, p.z], p.x), yr.at[2], yr.at[0], yr.at[1]], here)
            for s in range(1, 4):
                self.push(here, here, 9 + s, p.x_peer(s))

    def drain_sib(self):
        if self.sib_sent is not None:
            self.sib_sent.wait_send()
            self.sib_sent = None

    def drain(self):
        self.drain_sib()
        for copy in self.sent:
            copy.wait_send()
        self.sent = []


class ReduceSmall:
    def __init__(self, at, part, b, send, recv):
        self.p, self.part, self.b, self.send, self.recv = at, part, b, send, recv
        self.sent = []

    def push(self, src, dst, sem, peer):
        copy = remote(src, dst, self.send.at[sem], self.recv.at[sem], peer)
        copy.start()
        self.sent.append(copy)

    def arrive(self, ref, sem):
        remote(ref, ref, self.send.at[sem], self.recv.at[sem], self.p.sib).wait_recv()

    def step(self, n):
        p, b = self.p, self.b
        own, sibr, za, zb, yr, dr, out = (b[name] for name in ("own", "sib", "za", "zb", "yr", "dr", "out"))
        if n == 0:
            self.push(self.part.at[:, :, 1 - p.c], sibr, 0, p.sib)
        elif n == 1:
            self.arrive(sibr, 0)
            for yl in range(2):
                for z in range(4):
                    own[yl, z] = self.part[yl, z, p.c] + sibr[yl, z]
            self.push(own.at[:, p.z2, 0:24], za.at[0], 1, p.fore)
            self.push(own.at[:, p.z2, 24:48], za.at[1], 2, p.back)
        elif n == 2:
            self.arrive(za.at[0], 1)
            self.arrive(za.at[1], 2)
            for yl in range(2):
                own[yl, p.zp, 0:24] = own[yl, p.zp, 0:24] + za[0, yl]
                own[yl, p.zm, 24:48] = own[yl, p.zm, 24:48] + za[1, yl]
            self.push(own.at[:, p.zp], zb.at[0], 3, p.fore)
            self.push(own.at[:, p.zm], zb.at[1], 4, p.back)
        elif n == 3:
            self.arrive(zb.at[0], 3)
            self.arrive(zb.at[1], 4)
            for yl in range(2):
                own[yl, p.z] = own[yl, p.z] + zb[0, yl] + zb[1, yl]
            theirs = own.at[1 - p.yl, p.z]
            self.push(theirs.at[0:24], yr.at[0:24], 5, p.up)
            self.push(theirs.at[24:48], yr.at[24:48], 6, p.down)
        elif n == 4:
            self.arrive(yr.at[0:24], 5)
            self.arrive(yr.at[24:48], 6)
            dr[p.dp] = own[p.yl, p.z] + yr[...]
            for s in range(1, 8):
                self.push(dr.at[p.dp], dr.at[p.dp], 6 + s, p.dp_peer(s))
        elif n == 5:
            for s in range(1, 8):
                self.arrive(dr.at[lax.rem(p.dp + 8 - s, 8)], 6 + s)
            total = dr[0]
            for s in range(1, 8):
                total = total + dr[s]
            out[...] = total

    def drain(self):
        for copy in self.sent:
            copy.wait_send()


def sigmoid(v):
    return 0.5 * jnp.tanh(0.5 * v) + 0.5


def dot(a, b, dims=((1,), (0,))):
    return lax.dot_general(a, b, (dims, ((), ())), preferred_element_type=f32)


def lanes(start, size=128):
    return pl.ds(pl.multiple_of(start, 128), size)


def rows8(start, size):
    return pl.ds(pl.multiple_of(start, 8), size)


class Block:
    def __init__(self, b):
        self.b = b
        self.pad_rows = HALF * U

    def turn(self, to_frames):
        i = lax.broadcasted_iota(jnp.int32, (N, N), 0)
        k = lax.broadcasted_iota(jnp.int32, (N, N), 1)
        if not to_frames:
            i, k = k, i
        source = (i & (U - 1)) * L + lax.shift_right_logical(i, 3)
        return (k == source).astype(f32).astype(bf16)

    def setup(self):
        b = self.b
        b["turn"][...] = self.turn(True)
        b["back"][...] = self.turn(False)
        zero = jnp.zeros((self.pad_rows, TILE), f32)
        for ref in (b["gpad"].at[0], b["gpad"].at[1], b["cpad"]):
            ref[0 : self.pad_rows] = zero
            ref[self.pad_rows + N :] = zero
        b["rows"][...] = jnp.zeros((40, D), f32)

    def table(self):
        b = self.b
        for j in range(16):
            b["tab"][:, ROWS * j : ROWS * (j + 1)] = b["small"][j][0:40, 0:ROWS]

    def liveness(self):
        b = self.b
        limit = jnp.concatenate([b["lens"][u, 0:1, :] for u in range(U)], axis=0)

        @pl.loop(0, L)
        def _(l):
            b["live"][rows8(l * U, U), :] = (limit > l).astype(f32)

    def turn_in(self, name):
        ref, turn = self.b[name], self.b["turn"][...]
        for c in range(0, D, JOBW):
            ref[:, c : c + JOBW] = dot(turn, ref[:, c : c + JOBW]).astype(bf16)

    def norm(self):
        b = self.b

        @pl.loop(0, N // 32)
        def _(k):
            r = rows8(k * 32, 32)
            x = b["x"][r, :].astype(f32)
            mean = jnp.sum(x, axis=1, keepdims=True) * (1.0 / D)
            x = x - mean
            inverse = lax.rsqrt(jnp.sum(x * x, axis=1, keepdims=True) * (1.0 / D) + EPS)
            b["mean"][r, :] = jnp.broadcast_to(mean, (32, 128))
            b["inv"][r, :] = jnp.broadcast_to(inverse, (32, 128))
            b["normed"][r, :] = (x * inverse * b["tab"][31:32, :]).astype(bf16)

    def mask(self):
        b = self.b

        @pl.loop(0, N // 32)
        def _(k):
            r = rows8(k * 32, 32)
            b["masked"][r, :] = (b["g"][r, :].astype(f32) * b["live"][r, 0:1]).astype(bf16)

    def glu(self, t):
        b = self.b
        for q in range(2):
            r = slice(q * 256, (q + 1) * 256)
            out = dot(b["normed"][r, :], b["w"][t])
            for g in range(3):
                cols = slice(g * 128, (g + 1) * 128)
                value, sig = out[:, cols], sigmoid(out[:, TILE + g * 128 : TILE + (g + 1) * 128])
                b["a"][r, t * TILE + g * 128 : t * TILE + (g + 1) * 128] = value
                b["sig"][t % 2, r, cols] = sig
                live = (value * sig * b["live"][r, :]).astype(bf16).astype(f32)
                b["gpad"][t % 2, self.pad_rows + q * 256 : self.pad_rows + (q + 1) * 256, cols] = live

    def taps(self, ref, base, local, wide, flip):
        b = self.b
        window = [ref[rows8(base + 8 * i, 8), local] for i in range(SPAN)]
        sums = [jnp.zeros((8, 128), f32)] * SPAN
        for t in range(TAPS):
            row = TAPS - 1 - t if flip else t
            tap = jnp.broadcast_to(b["tab"][row : row + 1, wide], (8, 128))
            sums = [s + tap * v for s, v in zip(sums, window)]
            if t < TAPS - 1:
                window = window[1:] + [ref[rows8(base + 8 * (SPAN + t), 8), local]]
        return jnp.concatenate(sums, axis=0)

    def conv(self, t):
        b = self.b

        @pl.loop(0, 3 * (L // SPAN))
        def _(n):
            g, base = n // (L // SPAN), lax.rem(n, L // SPAN) * (SPAN * U)
            local, wide = lanes(g * 128), lanes(t * TILE + g * 128)
            out = self.taps(b["gpad"].at[t % 2], base, local, wide, False) + b["tab"][32:33, wide]
            sig = sigmoid(out)
            r = rows8(base, SPAN * U)
            b["swished"][r, wide] = (out * sig).astype(bf16)
            b["slope"][t % 2, r, local] = sig * (1.0 + out * (1.0 - sig))

    def encode(self, h, flush):
        b = self.b
        cols = slice(h * JOBW, (h + 1) * JOBW)
        for q in range(2):
            r = slice(q * 256, (q + 1) * 256)
            out = dot(b["swished"][r, :], b["p"][h])
            b["masked"][r, 0:JOBW] = (b["x"][r, cols].astype(f32) + out * b["live"][r, 0:1]).astype(bf16)
        for q in range(2):
            r = slice(q * 256, (q + 1) * 256)
            b["masked"][r, JOBW:D] = dot(b["back"][r, :], b["masked"][:, 0:JOBW]).astype(bf16)
        flush(h)

    def put(self, job, m, out, cols):
        mix = self.b["mix"]
        for q in range(4):
            j = 4 * m + q
            mix[job.slot(j % 2), j // 8, (j % 8) // 2, :, cols] = out[q * ROWS : (q + 1) * ROWS].astype(bf16)

    def project_part(self, h, job):
        b = self.b
        for m in range(4):
            out = dot(b["swished"][:, m * TILE : (m + 1) * TILE], b["masked"][:, h * JOBW : (h + 1) * JOBW], ((0,), (0,)))
            self.put(job, m, out, slice(0, JOBW))

    def back_project(self, t):
        b = self.b
        cols = slice(t * TILE, (t + 1) * TILE)
        for q in range(2):
            r = slice(q * 256, (q + 1) * 256)
            out = dot(b["masked"][r, 0:JOBW], b["p"][0, cols, :], ((1,), (1,)))
            out = out + dot(b["masked"][r, JOBW:D], b["p"][1, cols, :], ((1,), (1,)))
            b["cpad"][self.pad_rows + q * 256 : self.pad_rows + (q + 1) * 256, :] = out * b["slope"][t % 2, r, :]

    def tap_grads(self, t):
        b = self.b

        @pl.loop(0, 3)
        def _(g):
            local, wide = lanes(g * 128), lanes(t * TILE + g * 128)
            for first, count in ((0, 16), (16, 15)):

                def step(n, sums):
                    base = n * 64
                    ups = [b["cpad"][rows8(self.pad_rows + base + 8 * i, 8), local] for i in range(8)]
                    window = [b["gpad"][t % 2, rows8(base + 8 * (first + i), 8), local] for i in range(count)]
                    for i in range(8):
                        sums = [s + ups[i] * v for s, v in zip(sums[:count], window)] + sums[count:]
                        if i < 7:
                            window = window[1:] + [b["gpad"][t % 2, rows8(base + 8 * (first + count + i), 8), local]]
                    if first:
                        sums = sums[:count] + [sums[count] + ((ups[0] + ups[1]) + (ups[2] + ups[3])) + ((ups[4] + ups[5]) + (ups[6] + ups[7]))]
                    return sums

                extra = 1 if first else 0
                sums = lax.fori_loop(0, 8, step, [jnp.zeros((8, 128), f32)] * (count + extra))
                for i in range(count):
                    b["rows"][first + i : first + i + 1, wide] = jnp.sum(sums[i], axis=0, keepdims=True)
                if first:
                    b["rows"][32:33, wide] = jnp.sum(sums[count], axis=0, keepdims=True)

    def back_conv(self, t):
        b = self.b

        @pl.loop(0, 3 * (L // SPAN))
        def _(n):
            g, base = n // (L // SPAN), lax.rem(n, L // SPAN) * (SPAN * U)
            local, wide = lanes(g * 128), lanes(t * TILE + g * 128)
            r = rows8(base, SPAN * U)
            grad = self.taps(b["cpad"], base, local, wide, True) * b["live"][r, :]
            sig = b["sig"][t % 2, r, local]
            grad = grad * sig
            b["ge"][t, r, local] = grad.astype(bf16)
            b["ge"][t, r, lanes(TILE + g * 128)] = (grad * b["a"][r, wide] * (1.0 - sig)).astype(bf16)

    def expand_part(self, t, job):
        b = self.b
        for m in range(4):
            out = dot(b["normed"][:, m * TILE : (m + 1) * TILE], b["ge"][t], ((0,), (0,)))
            self.put(job, m, out, slice(0, JOBW))

    def grad_normed(self):
        b = self.b
        for q in range(2):
            r = slice(q * 256, (q + 1) * 256)
            for c in range(2):
                cols = slice(c * JOBW, (c + 1) * JOBW)
                out = dot(b["ge"][0, r, :], b["w"][0, cols, :], ((1,), (1,)))
                for t in range(1, TILES):
                    out = out + dot(b["ge"][t, r, :], b["w"][t, cols, :], ((1,), (1,)))
                b["a"][r, cols] = out

    def norm_back(self, q):
        b = self.b

        @pl.loop(0, 8)
        def _(k):
            r = rows8(q * 128 + k * 16, 16)
            gn = b["a"][r, :]
            inverse = b["inv"][r, 0:1]
            standard = (b["x"][r, :].astype(f32) - b["mean"][r, 0:1]) * inverse
            both = gn * standard
            b["gain8"][...] += both[0:8] + both[8:16]
            gain = b["tab"][31:32, :]
            h = gn * gain
            m1 = jnp.sum(h, axis=1, keepdims=True) * (1.0 / D)
            m2 = jnp.sum(both * gain, axis=1, keepdims=True) * (1.0 / D)
            grad = inverse * (h - m1 - standard * m2)
            b["normed"][r, :] = (b["g"][r, :].astype(f32) + grad).astype(bf16)

    def turn_out(self):
        b = self.b
        for c in range(0, D, JOBW):
            b["normed"][:, c : c + JOBW] = dot(b["back"][...], b["normed"][:, c : c + JOBW]).astype(bf16)


VMEM_NAMES = (
    ("x", (N, D), bf16), ("g", (N, D), bf16), ("lens", (U, 8, 128), jnp.int32), ("small", (16, 48, 128), f32),
    ("w", (TILES, D, JOBW), bf16), ("p", (2, D, JOBW), bf16),
    ("masked", (N, D), bf16), ("normed", (N, D), bf16), ("a", (N, D), f32), ("sig", (2, N, TILE), f32),
    ("slope", (2, N, TILE), f32), ("swished", (N, D), bf16), ("ge", (TILES, N, JOBW), bf16),
    ("gpad", (2, N + 2 * HALF * U, TILE), f32), ("cpad", (N + 2 * HALF * U, TILE), f32),
    ("live", (N, 128), f32), ("mean", (N, 128), f32), ("inv", (N, 128), f32),
    ("turn", (N, N), bf16), ("back", (N, N), bf16), ("tab", (40, D), f32), ("rows", (40, D), f32),
    ("gain8", (8, D), f32),
    ("mix", (OWN_RING + SEND_RING, 2, 4, ROWS, JOBW), bf16), ("sib", (JOBS, 2, 4, ROWS, JOBW), bf16),
    ("onex", (max(1, FIRST.count("x")), 3, 2, 4, 48, 384), bf16), ("onez", (max(1, FIRST.count("z")), 3, 2, ROWS, JOBW), bf16),
    ("two", (2, 3, 2, 48, 384), bf16), ("yr", (2, 3, 48, 384), bf16),
    ("yhalf", (max(1, FIRST.count("y")), 4, ROWS, JOBW), bf16), ("zr", (max(1, FIRST.count("y")), 3, ROWS, JOBW), bf16),
    ("xr", (max(1, FIRST.count("y")), 3, 48, 384), bf16), ("pr", (max(1, FIRST.count("y")), 48, 384), bf16),
    ("fin", (JOBS, ROWS, JOBW), bf16),
    ("spart", (2, 4, 2, 48, 128), f32), ("sown", (2, 4, 48, 128), f32), ("ssib", (2, 4, 48, 128), f32),
    ("sza", (2, 2, 24, 128), f32), ("szb", (2, 2, 48, 128), f32), ("syr", (48, 128), f32), ("sdr", (8, 48, 128), f32),
)
SEMS = (
    ("xs_", (4, 8)), ("xr_", (4, 8)), ("gs_", (7, 18)), ("gr_", (7, 18)), ("rs_", (JOBS, 14)), ("rr_", (JOBS, 14)),
    ("ss_", (14,)), ("sr_", (14,)), ("fill_", (12,)), ("enc_", (2,)),
)


def whole_kernel(frames, cot, lens, small, expand, project, o_enc, o_grad, o_small, o_expand, o_project, *scratch):
    b = dict(zip([n[0] for n in VMEM_NAMES + SEMS], scratch))
    at = Place()
    mine = pl.ds(pl.multiple_of(at.sh * ROWS, ROWS), ROWS)
    moves = [(small, b["small"].at[at.sh])]
    for t in range(TILES):
        for part in range(2):
            moves.append((expand.at[:, pl.ds(part * D + t * TILE, TILE)], b["w"].at[t, mine, pl.ds(part * TILE, TILE)]))
    for h in range(2):
        moves.append((project.at[:, pl.ds(h * JOBW, JOBW)], b["p"].at[h, mine, :]))
    fills = [pltpu.make_async_copy(s, d, b["fill_"].at[k]) for k, (s, d) in enumerate(moves)]
    for fill in fills:
        fill.start()
    at.greet()

    def slots(ref):
        return lambda q: ref.at[pl.ds(pl.multiple_of(q * L, L), L), :]

    def sems(k):
        return b["xs_"].at[k], b["xr_"].at[k]

    ex_len = Exchange(at, lambda q: lens.at[q], lambda q: b["lens"].at[q], *sems(0))
    for fill in fills:
        fill.wait()

    def block_small(j, start, size):
        return b["small"].at[j, pl.ds(start, size), :]

    def block_of(ref):
        return lambda j, start, size: ref.at[pl.ds(pl.multiple_of(j * ROWS + start, 48), size), :]

    gathers = [Gather(at, block_small, 48, b["gs_"], b["gr_"], 0)]
    order = (b["w"].at[0], b["w"].at[1], b["p"].at[0], b["p"].at[1], b["w"].at[2], b["w"].at[3])
    for k, ref in enumerate(order):
        gathers.append(Gather(at, block_of(ref), ROWS, b["gs_"], b["gr_"], 1 + k))
    for gather in gathers:
        gather.first()
    ex_x = Exchange(at, lambda q: frames.at[q], slots(b["x"]), *sems(1))
    clock = [0]
    begins = (0, 0, 2, 4, 6, 8, 10)

    def gather_wave():
        for gather, begin in zip(gathers, begins):
            if clock[0] >= begin:
                gather.advance()
        clock[0] += 1

    def gathered(k):
        while gathers[k].done < 6:
            gather_wave()

    block = Block(b)
    gather_wave()
    ex_g = Exchange(at, lambda q: cot.at[q], slots(b["g"]), *sems(2))
    gather_wave()
    block.setup()
    gather_wave()
    ex_len.wait()
    block.liveness()
    gather_wave()
    gather_wave()
    gathered(0)
    block.table()
    ex_x.wait()
    gather_wave()
    block.turn_in("x")
    gather_wave()
    block.norm()
    gather_wave()

    def out(k):
        if k in PROJECT_JOBS:
            h = PROJECT_JOBS.index(k)
            return [(slice(0, JOBW), o_project.at[:, h * JOBW : (h + 1) * JOBW])]
        t = EXPAND_JOBS.index(k)
        return [
            (slice(part * TILE, (part + 1) * TILE), o_expand.at[:, part * D + t * TILE : part * D + (t + 1) * TILE])
            for part in range(2)
        ]

    bufs = {**b, "out": out}
    jobs = []

    def job_for(k):
        job = Reduce(at, k, bufs, (b["rs_"], b["rr_"]))
        if k >= SEND_RING:
            jobs[k - SEND_RING].drain_sib()
        if k >= OWN_RING:
            jobs[k - OWN_RING].drain()
        return job

    def launch(job):
        job.advance()
        jobs.append(job)

    def wave():
        for job in reversed(jobs):
            job.advance()

    enc_out = []

    def flush(h):
        copy = pltpu.make_async_copy(b["masked"].at[:, pl.ds(JOBW, JOBW)], o_enc.at[:, pl.ds(h * JOBW, JOBW)], b["enc_"].at[h])
        copy.start()
        enc_out.append(copy)

    def forward(t):
        gathered((1, 2, 5, 6)[t])
        block.glu(t)
        gather_wave()
        block.conv(t)
        gather_wave()

    def backward(t):
        block.back_project(t)
        block.tap_grads(t)
        gather_wave()
        block.back_conv(t)
        gather_wave()
        wave()
        job = job_for(EXPAND_JOBS[t])
        block.expand_part(t, job)
        launch(job)

    forward(0)
    forward(1)
    ex_g.wait()
    block.turn_in("g")
    gathered(3)
    block.mask()
    gathered(4)
    backward(0)
    forward(2)
    backward(1)
    forward(3)
    for h in range(2):
        job = job_for(PROJECT_JOBS[h])
        block.project_part(h, job)
        launch(job)
    backward(2)
    backward(3)
    ex_x.drain()
    ex_g.drain()
    ex_len.drain()
    for gather in gathers:
        gather.drain()
    b["gain8"][...] = jnp.zeros((8, D), f32)
    block.grad_normed()
    wave()
    for q in range(4):
        block.norm_back(q)
    block.turn_out()
    ex_back = Exchange(at, slots(b["normed"]), lambda q: o_grad.at[q], *sems(3))
    b["rows"][31:32, :] = jnp.sum(b["gain8"][...], axis=0, keepdims=True)
    for j in range(16):
        values = b["rows"][:, ROWS * j : ROWS * (j + 1)].astype(bf16).astype(f32)
        b["spart"][j // 8, (j % 8) // 2, j % 2] = jnp.zeros((48, 128), f32)
        b["spart"][j // 8, (j % 8) // 2, j % 2, 0:40, 0:ROWS] = values
    tiny = ReduceSmall(
        at, b["spart"],
        {"own": b["sown"], "sib": b["ssib"], "za": b["sza"], "zb": b["szb"], "yr": b["syr"], "dr": b["sdr"], "out": o_small},
        b["ss_"], b["sr_"],
    )
    tiny.step(0)
    wave()
    for h in range(2):
        for copy in enc_out:
            copy.wait()
        block.encode(h, flush)
        wave()
        tiny.step(1 + h)
    enc_out[-1].wait()
    for n in range(3, 6):
        wave()
        tiny.step(n)
    while any(job.done < job.last for job in jobs):
        wave()
    ex_back.wait()
    ex_back.drain()
    tiny.drain()
    for job in jobs:
        job.drain()


def whole(frames, cot, lens, small, expand, project):
    any_spec = pl.BlockSpec(memory_space=pl.ANY)
    vmem = pl.BlockSpec(memory_space=pltpu.VMEM)
    return pl.pallas_call(
        whole_kernel,
        out_shape=[
            jax.ShapeDtypeStruct((N, D), bf16),
            jax.ShapeDtypeStruct((U, L, D), bf16),
            jax.ShapeDtypeStruct((48, 128), f32),
            jax.ShapeDtypeStruct((ROWS, 2 * D), f32),
            jax.ShapeDtypeStruct((ROWS, D), f32),
        ],
        in_specs=[any_spec] * 6,
        out_specs=[any_spec, any_spec, vmem, vmem, vmem],
        scratch_shapes=[pltpu.VMEM(s, d) for _, s, d in VMEM_NAMES] + [pltpu.SemaphoreType.DMA(s) for _, s in SEMS],
        compiler_params=pltpu.CompilerParams(
            collective_id=0, has_side_effects=True, vmem_limit_bytes=64 * 1024 * 1024 - 64 * 1024
        ),
    )(frames, cot, lens, small, expand, project)


def body(frames, cotangent, lengths, send_order, norm_gain, conv_bias, kernel, expand_weight, project_weight):
    count, length, width = frames.shape
    staged_frames = frames.at[send_order].get(mode="promise_in_bounds")
    staged_cot = cotangent.at[send_order].get(mode="promise_in_bounds")
    staged_len = jnp.broadcast_to(lengths.at[send_order].get(mode="promise_in_bounds")[:, None, None], (U, 8, 128))
    small = jnp.concatenate([kernel.T, norm_gain[None], conv_bias[None]], axis=0).astype(f32)
    small = jnp.pad(small, ((0, 48 - 33), (0, 128 - ROWS)))
    encoded, returned, g_small, g_expand, g_project = whole(
        staged_frames, staged_cot, staged_len, small, expand_weight, project_weight
    )
    plan = (send_order[None, :] == lax.broadcasted_iota(jnp.int32, (count, count), 0)).astype(bf16)
    frame_grad = jnp.einsum("kp,pfh->kfh", plan, returned, preferred_element_type=f32).astype(bf16)
    return (
        encoded.reshape(count, length, width), frame_grad,
        g_small[31, :ROWS], g_small[32, :ROWS], g_small[:31, :ROWS].T, g_expand, g_project,
    )


def solution(mesh):
    both, shard = P(("dp", "shard"), None, None), P("shard", None)
    return jax.shard_map(
        body,
        mesh=mesh,
        in_specs=(both, both, P(("dp", "shard")), P(("dp", "shard")), P("shard"), P("shard"), shard, shard, shard),
        out_specs=(both, both, P("shard"), P("shard"), shard, shard, shard),
        check_vma=False,
    )
```
